32 devices in a mesh: seq: 16 (over z, x, core), fsdp: 2 (over y).
Axes of the slice: x: 2, y: 2, z: 4, core: 2. Of those that a mesh axis runs over, the one named last changes fastest.
Arguments:
- prompt: bfloat16 [2, 256, 4096], P('fsdp'), may hold values from -6 to 6
- lengths: int32 [2], P('fsdp'), may hold values from 1 to 256, 384 in all
- timesteps: int32 [2], P('fsdp'), may hold values from 0 to 999
- ref_errors: float32 [2, 2], P('fsdp'), may hold values from 4.2 to 4.45
- gain_ffn: float32 [4096], replicated, may hold values from 0.5 to 1.5
- w_in_gate: bfloat16 [4096, 8192], P('fsdp', 'seq'), may hold values from -0.09375 to 0.09375
- w_in_up: bfloat16 [4096, 8192], P('fsdp', 'seq'), may hold values from -0.09375 to 0.09375
- w_in_down: bfloat16 [8192, 4096], P('seq', 'fsdp'), may hold values from -0.0625 to 0.0625
- gain_final: float32 [4096], replicated, may hold values from 0.5 to 1.5
- w_context: bfloat16 [4096, 2048], P('fsdp', 'seq'), may hold values from -0.09375 to 0.09375
- image_q: bfloat16 [2, 2, 1024, 1024], P('fsdp', None, 'seq'), may hold values from -128 to 128
- image_k: bfloat16 [2, 2, 1024, 1024], P('fsdp', None, 'seq'), may hold values from -4 to 4
- image_v: bfloat16 [2, 2, 1024, 1024], P('fsdp', None, 'seq'), may hold values from -6 to 6
- w_out: bfloat16 [1024, 1280], P('fsdp'), may hold values from -0.1875 to 0.1875
- target: bfloat16 [2, 2, 1024, 1280], P('fsdp', None, 'seq'), may hold values from -12 to 12
Outputs:
- pair_loss: float32 [2], P('fsdp')
- grad_q: bfloat16 [2, 2, 1024, 1024], P('fsdp', None, None, 'seq')
- grad_k: bfloat16 [2, 2, 1024, 1024], P('fsdp', None, None, 'seq')
- grad_v: bfloat16 [2, 2, 1024, 1024], P('fsdp', None, None, 'seq')
The draws below stay inside these ranges and needn't reach their ends.
All inputs are finite; a program needn't handle non-finite values. No bound on the sum of `lengths` on one device may be relied on, other than what follows from the above.
Results may differ from the reference program's by a relative error of at most 0.029.
Values may be sent and summed in bfloat16 or wider, within the bound.
No kernel may reach another device: no remote copies, remote signals or barrier semaphores. Data moves between devices by JAX's collectives and lax.ppermute only.
A program may use at most 128 MiB of HBM per device.

```python
import math
import jax
import jax.numpy as jnp
import numpy as np
from jax import lax

D_ENC = 4096
FF = 8192
PROMPT = 256
HEAD = 64
CH = 1280
SEQ = 1024
HEADS = 16
INNER = 1024
PAIRS = 2


def attention_draw(key):
    base_key = jax.random.fold_in(key, 7)
    key_query, key_keys = jax.random.split(base_key, 2)
    full_shape = (PAIRS, 2, SEQ, INNER)
    key_vals = jnp.clip(jax.random.normal(key_keys, full_shape, jnp.float32), -4.0, 4.0)
    query_vals = 1.5 * jnp.clip(jax.random.normal(key_query, full_shape, jnp.float32), -4.0, 4.0)
    return (query_vals, key_vals)


def draw_image_q(key, part):
    return attention_draw(key)[0].astype(jnp.bfloat16)


def draw_image_k(key, part):
    return attention_draw(key)[1].astype(jnp.bfloat16)


def draw_target(key, part):
    base_key = jax.random.fold_in(key, 11)
    key_noise = jax.random.fold_in(base_key, 0)
    position_ramp = 1.0 + 2.0 * jnp.arange(SEQ, dtype=jnp.float32) / (SEQ - 1)
    noise_vals = jnp.clip(jax.random.normal(key_noise, (PAIRS, 2, SEQ, CH), jnp.float32), -4.0, 4.0)
    return (noise_vals * position_ramp[None, None, :, None]).astype(jnp.bfloat16)


def level_of(key, dims, cuts, smallest, largest):
    def one(axis_at, parts):
        heights = jax.random.uniform(jax.random.fold_in(jax.random.fold_in(key, 6), axis_at), (parts,), jnp.float32, smallest / len(cuts), largest / len(cuts))
        return jnp.repeat(jnp.exp(heights), dims[axis_at] // parts).reshape((-1,) + (1,) * (len(dims) - axis_at - 1))

    loudness = one(*cuts[0])
    for cut in cuts[1:]:
        loudness = loudness * one(*cut)
    return loudness


def profile(number_of, total, limit, lean):
    loads = [(1 << 20) // math.isqrt(standing ** lean) + 1 for standing in range(2, number_of + 1)]
    spare, counts = total - limit - (number_of - 1), [1] * (number_of - 1)
    while spare > 0:
        candidates = [i for i in range(number_of - 1) if counts[i] < limit]
        mass, left = sum([loads[i] for i in candidates]), spare
        for i in candidates:
            more = min(limit - counts[i], max(1, left * loads[i] // mass), spare)
            counts[i] = counts[i] + more
            spare = spare - more
    return np.array([limit] + counts)


def uneven(key, amount, total, bound, lean):
    if amount == 2:
        one = jax.random.randint(key, (), max(1, total - bound), min(bound, total - 1) + 1)
        return jnp.stack([one, total - one])
    sizes = jnp.asarray(profile(amount, total, bound, lean), jnp.int32)
    couples = (amount - 1) // 2
    giver, receiver = sizes[1:1 + 2 * couples:2], sizes[2:2 + 2 * couples:2]
    room = jnp.minimum(giver - 1, bound - receiver)
    moved = jax.random.randint(jax.random.fold_in(key, 1), (couples,), 0, 1 << 20) % (room + 1)
    sizes = sizes.at[1:1 + 2 * couples:2].set(giver - moved).at[2:2 + 2 * couples:2].set(receiver + moved)
    return sizes[jax.random.permutation(jax.random.fold_in(key, 2), amount)]


def centred(key, extent, spread, limit, shards=(), kind=jnp.bfloat16):
    factor_of = level_of(key, extent, shards, -0.22, 0.18) if shards else 1.0
    result = jax.random.normal(key, extent, jnp.float32) * spread * factor_of
    return jnp.minimum(jnp.maximum(result, -limit), limit).astype(kind)


def setup_inputs(seed: int = 0) -> dict:
    key_of = jax.random.split(jax.random.key(seed), 16)
    return {
        "prompt": centred(key_of[0], (PAIRS, PROMPT, D_ENC), 1.0, 6.0, ((0, 2),)),
        "lengths": uneven(key_of[1], PAIRS, PROMPT * (PAIRS + 1) // 2, PROMPT, 0).astype(jnp.int32),
        "timesteps": jax.random.randint(key_of[2], (PAIRS,), 0, 1000).astype(jnp.int32),
        "ref_errors": jnp.clip(4.2 + 0.25 * jax.random.uniform(key_of[3], (PAIRS, 2), jnp.float32) ** level_of(key_of[3], (PAIRS, 2), ((0, 2),), -0.2, 0.2), 4.2, 4.45),
        "gain_ffn": jnp.clip(1.0 + 0.1 * jax.random.normal(key_of[4], (D_ENC,), jnp.float32), 0.5, 1.5),
        "w_in_gate": centred(key_of[5], (D_ENC, FF), D_ENC ** -0.5, 0.09375, ((0, 2), (1, 16))),
        "w_in_up": centred(key_of[6], (D_ENC, FF), D_ENC ** -0.5, 0.09375, ((0, 2), (1, 16))),
        "w_in_down": centred(key_of[7], (FF, D_ENC), FF ** -0.5, 0.0625, ((0, 16), (1, 2))),
        "gain_final": jnp.clip(1.0 + 0.1 * jax.random.normal(key_of[8], (D_ENC,), jnp.float32), 0.5, 1.5),
        "w_context": centred(key_of[9], (D_ENC, 2 * INNER), D_ENC ** -0.5, 0.09375, ((0, 2), (1, 16))),
        "image_q": draw_image_q(jax.random.fold_in(key_of[15], 71), 0),
        "image_k": draw_image_k(jax.random.fold_in(key_of[15], 71), 0),
        "image_v": centred(key_of[12], (PAIRS, 2, SEQ, INNER), 1.0, 6.0, ((0, 2), (2, 16))),
        "w_out": centred(key_of[13], (INNER, CH), INNER ** -0.5, 0.1875, ((0, 2),)),
        "target": draw_target(jax.random.fold_in(key_of[15], 71), 0),
    }


dpo_beta = 20.0
norm_eps = 1e-06

def rms_gain(values, gain):
    mean_sq = lax.optimization_barrier(jnp.mean(values * values, axis=-1, keepdims=True))
    return values * lax.rsqrt(mean_sq + norm_eps) * gain

def noise_level(step_index):
    fraction = (step_index.astype(jnp.float32) + 1.0) / 1000.0
    return 3.0 * fraction / (1.0 + 2.0 * fraction)

def softmax_rows(queries, key_rows, key_mask):
    scores = jnp.dot(queries, key_rows.T, preferred_element_type=jnp.float32) * (1.0 / math.sqrt(HEAD))
    scores = jnp.where(key_mask[None, :], scores, -jnp.inf)
    top_score = lax.optimization_barrier(jnp.max(scores, axis=-1, keepdims=True))
    weights = jnp.exp(scores - top_score)
    return (weights / lax.optimization_barrier(jnp.sum(weights, axis=-1, keepdims=True))).astype(jnp.bfloat16)

def head_forward(queries, key_rows, value_rows, key_mask):
    probs_bf = softmax_rows(queries, key_rows, key_mask)
    return jnp.dot(probs_bf, value_rows, preferred_element_type=jnp.float32).astype(jnp.bfloat16)

def head_backward(queries, key_rows, value_rows, key_mask, attended, grad_out):
    seq_len = queries.shape[0]
    probs_bf = softmax_rows(queries, key_rows, key_mask)
    grad_prob = jnp.dot(grad_out, value_rows.T, preferred_element_type=jnp.float32)
    row_delta = lax.optimization_barrier(jnp.sum(grad_out.astype(jnp.float32) * attended.astype(jnp.float32), axis=-1, keepdims=True))
    grad_score = (probs_bf.astype(jnp.float32) * (grad_prob - row_delta) * (1.0 / math.sqrt(HEAD))).astype(jnp.bfloat16)
    grad_query = jnp.dot(grad_score, key_rows, preferred_element_type=jnp.float32).astype(jnp.bfloat16)
    grad_key = jnp.dot(grad_score[:, :seq_len].T, queries, preferred_element_type=jnp.float32).astype(jnp.bfloat16)
    grad_value = jnp.dot(probs_bf[:, :seq_len].T, grad_out, preferred_element_type=jnp.float32).astype(jnp.bfloat16)
    return (grad_query, grad_key, grad_value)

def encode(prompt_rows, gain_ffn, w_in_gate, w_in_up, w_in_down, gain_final, w_context):
    prompt_f32 = prompt_rows.astype(jnp.float32)
    normed = rms_gain(prompt_f32, gain_ffn).astype(jnp.bfloat16)
    gate_act = jnp.dot(normed, w_in_gate, preferred_element_type=jnp.float32)
    up_act = jnp.dot(normed, w_in_up, preferred_element_type=jnp.float32)
    hidden = (jax.nn.gelu(gate_act, approximate=True) * up_act).astype(jnp.bfloat16)
    state = prompt_f32 + jnp.dot(hidden, w_in_down, preferred_element_type=jnp.float32)
    encoded = rms_gain(state, gain_final).astype(jnp.bfloat16)
    return jnp.dot(encoded, w_context, preferred_element_type=jnp.float32).astype(jnp.bfloat16)

def split_heads(rows):
    return jnp.transpose(rows.reshape(SEQ, HEADS, HEAD), (1, 0, 2))

def join_heads(rows):
    return jnp.transpose(rows, (1, 0, 2)).reshape(SEQ, INNER)

def reference(prompt, lengths, timesteps, ref_errors, gain_ffn, w_in_gate, w_in_up, w_in_down, gain_final, w_context, image_q, image_k, image_v, w_out, target):

    def one_pair(inputs):
        prompt_rows, length, step_index, ref_pair, pair_q, pair_k, pair_v, pair_target = inputs
        context = encode(prompt_rows, gain_ffn, w_in_gate, w_in_up, w_in_down, gain_final, w_context)
        context = context.reshape(PROMPT, HEADS, 2, HEAD)
        text_keys = jnp.transpose(context[:, :, 0, :], (1, 0, 2))
        text_values = jnp.transpose(context[:, :, 1, :], (1, 0, 2))
        key_mask = jnp.arange(SEQ + PROMPT) < SEQ + length
        head_sets = []
        attended_all = []
        residuals = []
        errors = []
        for stream in range(2):
            q_heads = split_heads(pair_q[stream])
            k_heads = jnp.concatenate([split_heads(pair_k[stream]), text_keys], axis=1)
            v_heads = jnp.concatenate([split_heads(pair_v[stream]), text_values], axis=1)

            def forward_head(head_items):
                q_one, k_one, v_one = head_items
                return head_forward(q_one, k_one, v_one, key_mask)
            head_outs = lax.map(forward_head, (q_heads, k_heads, v_heads))
            predicted = jnp.dot(join_heads(head_outs), w_out, preferred_element_type=jnp.float32)
            residual = predicted - pair_target[stream].astype(jnp.float32)
            head_sets.append((q_heads, k_heads, v_heads))
            attended_all.append(head_outs)
            residuals.append(residual)
            errors.append(jnp.mean(residual * residual))
        error_gap = errors[0] - ref_pair[0] - (errors[1] - ref_pair[1])
        sigma_t = noise_level(step_index)
        logit_value = dpo_beta * sigma_t * error_gap
        pair_loss = jax.nn.softplus(logit_value)
        coefficient = sigma_t * jax.nn.sigmoid(logit_value)
        grad_sets = []
        for stream in range(2):
            signed = coefficient if stream == 0 else -coefficient
            grad_pred = (signed * residuals[stream]).astype(jnp.bfloat16)
            grad_tok = jnp.dot(grad_pred, w_out.T, preferred_element_type=jnp.float32).astype(jnp.bfloat16)
            q_heads, k_heads, v_heads = head_sets[stream]

            def backward_head(head_items):
                q_one, k_one, v_one, out_one, grad_one = head_items
                return head_backward(q_one, k_one, v_one, key_mask, out_one, grad_one)
            grad_query, grad_key, grad_value = lax.map(backward_head, (q_heads, k_heads, v_heads, attended_all[stream], split_heads(grad_tok)))
            grad_sets.append((join_heads(grad_query), join_heads(grad_key), join_heads(grad_value)))
        grad_query = jnp.stack([grad_sets[0][0], grad_sets[1][0]])
        grad_key = jnp.stack([grad_sets[0][1], grad_sets[1][1]])
        grad_value = jnp.stack([grad_sets[0][2], grad_sets[1][2]])
        return (pair_loss, grad_query, grad_key, grad_value)
    results = lax.map(one_pair, (prompt, lengths, timesteps, ref_errors, image_q, image_k, image_v, target))
    return (results[0], results[1], results[2], results[3])
```

```python
import math

import jax
import jax.numpy as jnp
from jax import lax
from jax.experimental import pallas as pl
from jax.experimental.pallas import tpu as pltpu
from jax.sharding import PartitionSpec as P

HEAD = 64
LANES = 128
f32 = jnp.float32
bf16 = jnp.bfloat16

dpo_beta = 20.0
norm_eps = 1e-06
inv_root = 1.0 / math.sqrt(HEAD)


def noise_level(step_index):
    fraction = (step_index.astype(f32) + 1.0) / 1000.0
    return 3.0 * fraction / (1.0 + 2.0 * fraction)


def dot(a, b):
    return jnp.dot(a, b, preferred_element_type=f32)


def dot_nt(a, b):
    return lax.dot_general(a, b, (((1,), (1,)), ((), ())), preferred_element_type=f32)


def dot_tn(a, b):
    return lax.dot_general(a, b, (((0,), (0,)), ((), ())), preferred_element_type=f32)


def swap(x, axis, size, mask):
    return lax.ppermute(x, axis, [(i, i ^ mask) for i in range(size)])


def vmem():
    return pl.BlockSpec(memory_space=pltpu.VMEM)


def smem():
    return pl.BlockSpec(memory_space=pltpu.SMEM)


params = pltpu.CompilerParams(vmem_limit_bytes=48 * 1024 * 1024)


def pack_kernel(q_ref, k_ref, v_ref, out_ref):
    tok = q_ref.shape[1]
    for n, ref in enumerate((q_ref, k_ref, v_ref)):
        for pair in range(ref.shape[2] // LANES):
            a = ref[0, :, pair * LANES : (pair + 1) * LANES]
            b = ref[1, :, pair * LANES : (pair + 1) * LANES]
            rows = slice(n * tok, (n + 1) * tok)
            out_ref[2 * pair, rows, :] = jnp.concatenate([a[:, :HEAD], b[:, :HEAD]], axis=1)
            out_ref[2 * pair + 1, rows, :] = jnp.concatenate([a[:, HEAD:], b[:, HEAD:]], axis=1)


def pack_heads(q, k, v):
    tok, inner = q.shape[1], q.shape[2]
    return pl.pallas_call(
        pack_kernel,
        out_shape=jax.ShapeDtypeStruct((inner // HEAD, 3 * tok, LANES), bf16),
        in_specs=[vmem()] * 3,
        out_specs=vmem(),
        compiler_params=params,
        name="pack_heads",
    )(q, k, v)


def down_kernel(idx_ref, hid_ref, w_ref, out_ref):
    hidden = hid_ref[...]
    for p in range(out_ref.shape[0]):
        start = pl.multiple_of(idx_ref[p] * LANES, LANES)
        out_ref[p] = dot(hidden, w_ref[:, pl.ds(start, LANES)]).astype(bf16)


def down_product(idx, hidden, w_down):
    blocks = w_down.shape[1] // LANES
    return pl.pallas_call(
        down_kernel,
        out_shape=jax.ShapeDtypeStruct((blocks, hidden.shape[0], LANES), bf16),
        in_specs=[smem(), vmem(), vmem()],
        out_specs=vmem(),
        compiler_params=params,
        name="down_product",
    )(idx, hidden, w_down)


def context_kernel(idx_ref, y_ref, pp_ref, gain_ref, w_ref, ctx_ref, sq_ref):
    blocks, rows = y_ref.shape[0], y_ref.shape[1]
    acc = jnp.zeros((rows, w_ref.shape[1]), f32)
    sq = jnp.zeros((rows, LANES), f32)
    for p in range(blocks):
        start = pl.multiple_of(idx_ref[p] * LANES, LANES)
        state = y_ref[p].astype(f32) + pp_ref[:, pl.ds(start, LANES)].astype(f32)
        sq = sq + state * state
        scaled = (state * gain_ref[:, pl.ds(start, LANES)]).astype(bf16)
        acc = acc + dot(scaled, w_ref[pl.ds(start, LANES), :])
    ctx_ref[...] = acc.astype(bf16)
    sq_ref[...] = jnp.sum(sq.T, axis=0, keepdims=True)


def context_product(idx, y, packed_prompt, gain, w_context):
    rows = y.shape[1]
    return pl.pallas_call(
        context_kernel,
        out_shape=(
            jax.ShapeDtypeStruct((rows, w_context.shape[1]), bf16),
            jax.ShapeDtypeStruct((1, rows), f32),
        ),
        in_specs=[smem(), vmem(), vmem(), vmem(), vmem()],
        out_specs=(vmem(), vmem()),
        compiler_params=params,
        name="context_product",
    )(idx, y, packed_prompt, gain, w_context)


def bit_reversed(size):
    bits = size.bit_length() - 1
    return [int(format(p, "b").zfill(bits)[::-1], 2) if bits else 0 for p in range(size)]


def seq_sum(x, size):
    masks = [1 << b for b in range(size.bit_length() - 1)]
    for mask in masks:
        half = x.shape[0] // 2
        got = swap(x[half:], "seq", size, mask)
        x = (x[:half].astype(f32) + got.astype(f32)).astype(bf16)
    for mask in reversed(masks):
        x = jnp.concatenate([x, swap(x, "seq", size, mask)], axis=0)
    return x


def encode_shared(
    S, prompt, lengths, gain_ffn, w_gate, w_up, w_down, gain_final, w_context
):
    s = lax.axis_index("seq")
    f = lax.axis_index("fsdp")
    own = prompt[0]
    rows, width = own.shape
    cols = width // 2
    half = rows // 2
    core = s & 1

    away = lax.dynamic_slice(own, (core * half, (1 - f) * cols), (half, cols))
    got_a = swap(away, "fsdp", 2, 1)
    other_len = swap(lengths, "fsdp", 2, 1)[0]
    own_f32 = own.astype(f32)
    scale = lax.rsqrt(jnp.mean(own_f32 * own_f32, axis=-1) + norm_eps)
    other_scale = swap(scale.reshape(-1, LANES), "fsdp", 2, 1).reshape(-1)
    got_b = swap(got_a, "seq", S, 1)
    gain = lax.dynamic_slice(gain_ffn, (f * cols,), (cols,))

    here = lax.dynamic_slice(own, (0, f * cols), (rows, cols))
    first = core * half
    scale_a = lax.dynamic_slice(other_scale, (first,), (half,))
    scale_b = lax.dynamic_slice(other_scale, (half - first,), (half,))

    def partial_of(raw, row_scale):
        normed = (raw.astype(f32) * row_scale[:, None] * gain[None, :]).astype(bf16)
        return jnp.concatenate(
            [dot(normed, w_gate).astype(bf16), dot(normed, w_up).astype(bf16)], axis=1
        )

    own_len = lengths[0]
    own_start = jnp.where(f == 0, 0, other_len)
    other_start = jnp.where(f == 0, own_len, 0)
    row = jnp.arange(half, dtype=jnp.int32)
    source = jnp.concatenate([row, row + half, row + first, row + half - first])
    is_own = jnp.arange(2 * rows) < rows
    place = source + jnp.where(is_own, own_start, other_start)
    place = jnp.where(source < jnp.where(is_own, own_len, other_len), place, -1)
    total = rows * 3 // 2
    select = (jnp.arange(total)[:, None] == place[None, :]).astype(bf16)

    parts = jnp.concatenate(
        [partial_of(here, scale), partial_of(got_a, scale_a), partial_of(got_b, scale_b)], axis=0
    )
    packed = dot(select, parts).astype(bf16)
    both = packed.astype(f32) + swap(packed, "fsdp", 2, 1).astype(f32)
    units = w_gate.shape[1]
    hidden = (jax.nn.gelu(both[:, :units], approximate=True) * both[:, units:]).astype(bf16)

    packed_prompt = dot(select, jnp.concatenate([here, got_a, got_b], axis=0)).astype(bf16)
    idx = jnp.array(bit_reversed(S), jnp.int32) ^ s
    y = down_product(idx, hidden, w_down)
    y = seq_sum(y, S)
    gain_here = lax.dynamic_slice(gain_final, (f * cols,), (cols,))[None]
    ctx, sq = context_product(idx, y, packed_prompt, gain_here, w_context)
    ctx_other = swap(ctx, "fsdp", 2, 1)
    sq_other = swap(sq, "fsdp", 2, 1)
    inv = lax.rsqrt((sq + sq_other)[0] / width + norm_eps)
    ctx = ((ctx.astype(f32) + ctx_other.astype(f32)) * inv[:, None]).astype(bf16)
    return dot_tn(select[:, :rows], ctx).astype(bf16)


def rms_gain(values, gain):
    mean_sq = jnp.mean(values * values, axis=-1, keepdims=True)
    return values * lax.rsqrt(mean_sq + norm_eps) * gain


def encode_gathered(prompt, gain_ffn, w_gate, w_up, w_down, gain_final, w_context):
    gate_full = lax.all_gather(w_gate, "fsdp", axis=0, tiled=True)
    up_full = lax.all_gather(w_up, "fsdp", axis=0, tiled=True)
    down_full = lax.all_gather(w_down, "fsdp", axis=1, tiled=True)
    context_full = lax.all_gather(w_context, "fsdp", axis=0, tiled=True)
    prompt_f32 = prompt[0].astype(f32)
    normed = rms_gain(prompt_f32, gain_ffn).astype(bf16)
    hidden = (
        jax.nn.gelu(dot(normed, gate_full), approximate=True) * dot(normed, up_full)
    ).astype(bf16)
    summed = lax.psum(dot(hidden, down_full).astype(bf16), "seq").astype(f32)
    encoded = rms_gain(prompt_f32 + summed, gain_final).astype(bf16)
    return dot(encoded, context_full).astype(bf16)


def lanes_of(stream):
    return slice(stream * HEAD, (stream + 1) * HEAD)


def rows_of(ref):
    value = ref[...]
    return value.reshape(-1, LANES)


def image_kernel(q_ref, k_ref, v_ref, e_ref, o_ref, m_ref, l_ref):
    q, k, v = rows_of(q_ref), rows_of(k_ref), rows_of(v_ref)
    rows = q.shape[0]
    outs, tops, sums = [], [], []
    for stream in range(2):
        at = lanes_of(stream)
        scores = dot_nt(q[:, at] * jnp.asarray(inv_root, bf16), k[:, at])
        top = jnp.max(scores, axis=-1, keepdims=True)
        e = jnp.exp(scores - top)
        eb = e.astype(bf16)
        e_ref[stream] = eb
        outs.append(dot(eb, v[:, at]))
        tops.append(jnp.broadcast_to(top, (rows, HEAD)))
        sums.append(jnp.broadcast_to(jnp.sum(e, axis=-1, keepdims=True), (rows, HEAD)))
    o_ref[...] = jnp.concatenate(outs, axis=1)
    m_ref[...] = jnp.concatenate(tops, axis=1)
    l_ref[...] = jnp.concatenate(sums, axis=1)


def q_blocks(S, tok):
    rows = min(256, S * tok)
    return rows // tok, S * tok // rows, rows


def image_part(qkv):
    S, _, tok, _ = qkv.shape
    group, steps, rows = q_blocks(S, tok)
    seq_len = S * tok
    whole = lambda n: pl.BlockSpec((S, None, tok, LANES), lambda i: (0, n, 0, 0))
    flat = pl.BlockSpec((rows, LANES), lambda i: (i, 0))
    return pl.pallas_call(
        image_kernel,
        grid=(steps,),
        out_shape=(jax.ShapeDtypeStruct((2, seq_len, seq_len), bf16),)
        + (jax.ShapeDtypeStruct((seq_len, LANES), f32),) * 3,
        in_specs=[
            pl.BlockSpec((group, None, tok, LANES), lambda i: (i, 0, 0, 0)),
            whole(1),
            whole(2),
        ],
        out_specs=(pl.BlockSpec((2, rows, seq_len), lambda i: (0, i, 0)), flat, flat, flat),
        compiler_params=params,
        name="image_part",
    )(qkv, qkv, qkv)


def text_kernel(len_ref, q_ref, ctx_ref, o_ref, m_ref, l_ref, out_ref, p_ref, c_ref):
    q = rows_of(q_ref)
    ctx = ctx_ref[...]
    keys, values = ctx[:, :HEAD], ctx[:, HEAD:]
    keep = lax.broadcasted_iota(jnp.int32, (q.shape[0], ctx.shape[0]), 1) < len_ref[0]
    outs, scales = [], []
    for stream in range(2):
        at = lanes_of(stream)
        scores = dot_nt(q[:, at] * jnp.asarray(inv_root, bf16), keys)
        scores = jnp.where(keep, scores, -jnp.inf)
        top_image = m_ref[:, stream * HEAD : stream * HEAD + 1]
        top = jnp.maximum(top_image, jnp.max(scores, axis=-1, keepdims=True))
        e = jnp.exp(scores - top)
        shrink = jnp.exp(top_image - top)
        total = l_ref[:, stream * HEAD : stream * HEAD + 1] * shrink + jnp.sum(
            e, axis=-1, keepdims=True
        )
        inv = 1.0 / total
        probs = (e * inv).astype(bf16)
        p_ref[stream] = probs
        scale = shrink * inv
        outs.append(o_ref[:, at] * scale + dot(probs, values))
        scales.append(jnp.broadcast_to(scale, (q.shape[0], HEAD)))
    out = jnp.concatenate(outs, axis=1).astype(bf16)
    out_ref[...] = out.reshape(out_ref.shape)
    c_ref[...] = jnp.concatenate(scales, axis=1)


def text_part(lengths, qkv, ctx, o_img, m_img, l_img):
    S, _, tok, _ = qkv.shape
    group, steps, rows = q_blocks(S, tok)
    seq_len = S * tok
    text = ctx.shape[0]
    flat = pl.BlockSpec((rows, LANES), lambda i: (i, 0))
    return pl.pallas_call(
        text_kernel,
        grid=(steps,),
        out_shape=(
            jax.ShapeDtypeStruct((S, tok, LANES), bf16),
            jax.ShapeDtypeStruct((2, seq_len, text), bf16),
            jax.ShapeDtypeStruct((seq_len, LANES), f32),
        ),
        in_specs=[
            smem(),
            pl.BlockSpec((group, None, tok, LANES), lambda i: (i, 0, 0, 0)),
            pl.BlockSpec((text, LANES), lambda i: (0, 0)),
            flat,
            flat,
            flat,
        ],
        out_specs=(
            pl.BlockSpec((group, tok, LANES), lambda i: (i, 0, 0)),
            pl.BlockSpec((2, rows, text), lambda i: (0, i, 0)),
            flat,
        ),
        compiler_params=params,
        name="text_part",
    )(lengths, qkv, ctx, o_img, m_img, l_img)


def project_kernel(idx_ref, o_ref, target_ref, *refs):
    counts = len(refs) - 3
    w_refs, out_ref, err_ref, a_ref = refs[:counts], refs[-3], refs[-2], refs[-1]
    heads, tok = o_ref.shape[0], o_ref.shape[1]
    blocks, _, block_rows = a_ref.shape
    pairs = block_rows // LANES
    for pair in range(heads // 2):
        a, b = o_ref[2 * pair], o_ref[2 * pair + 1]
        at = slice((pair % pairs) * LANES, (pair % pairs + 1) * LANES)
        a_ref[pair // pairs, :tok, at] = jnp.concatenate([a[:, :HEAD], b[:, :HEAD]], axis=1)
        a_ref[pair // pairs, tok:, at] = jnp.concatenate([a[:, HEAD:], b[:, HEAD:]], axis=1)
    slots = []
    for ref in w_refs:
        for n in range(ref.shape[0] // block_rows):
            slots.append((ref, n * block_rows))
    pred = None
    for slot, (ref, start) in enumerate(slots):
        term = dot(a_ref[idx_ref[slot]], ref[start : start + block_rows, :])
        pred = term if pred is None else pred + term
    target = target_ref[...].reshape(2 * tok, -1).astype(f32)
    residual = pred - target
    squares = residual * residual
    for stream in range(2):
        part = squares[stream * tok : (stream + 1) * tok]
        total = jnp.sum(jnp.sum(part, axis=0, keepdims=True), axis=1, keepdims=True)
        err_ref[stream : stream + 1, :] = jnp.broadcast_to(total, (1, LANES))
    grad = residual.astype(bf16)
    for slot, (ref, start) in enumerate(slots):
        g = dot_nt(grad, ref[start : start + block_rows, :]).astype(bf16)
        head = idx_ref[slot] * (2 * pairs)
        for pair in range(pairs):
            a = g[:tok, pair * LANES : (pair + 1) * LANES]
            b = g[tok:, pair * LANES : (pair + 1) * LANES]
            out_ref[head + 2 * pair] = jnp.concatenate([a[:, :HEAD], b[:, :HEAD]], axis=1)
            out_ref[head + 2 * pair + 1] = jnp.concatenate([a[:, HEAD:], b[:, HEAD:]], axis=1)


def project(idx, attended, target, weights):
    S, tok, _ = attended.shape
    blocks = idx.shape[0]
    block_rows = sum(w.shape[0] for w in weights) // blocks
    return pl.pallas_call(
        project_kernel,
        out_shape=(
            jax.ShapeDtypeStruct((S, tok, LANES), bf16),
            jax.ShapeDtypeStruct((2, LANES), f32),
        ),
        in_specs=[smem()] + [vmem()] * (2 + len(weights)),
        out_specs=(vmem(), vmem()),
        scratch_shapes=[pltpu.VMEM((blocks, 2 * tok, block_rows), bf16)],
        compiler_params=params,
        name="project",
    )(idx, attended, target, *weights)


def backward_kernel(
    coef_ref, q_ref, k_ref, v_ref, ctx_ref, e_ref, p_ref, c_ref, o_ref, g_ref,
    dq_ref, dk_ref, dv_ref, ka_ref, va_ref,
):
    step = pl.program_id(0)
    q, k, v = rows_of(q_ref), rows_of(k_ref), rows_of(v_ref)
    o, g = rows_of(o_ref), rows_of(g_ref)
    ctx = ctx_ref[...]
    keys, values = ctx[:, :HEAD], ctx[:, HEAD:]
    products = g.astype(f32) * o.astype(f32)

    @pl.when(step == 0)
    def _():
        ka_ref[...] = jnp.zeros_like(ka_ref)
        va_ref[...] = jnp.zeros_like(va_ref)

    for stream in range(2):
        at = lanes_of(stream)
        gs = g[:, at]
        delta = jnp.sum(products[:, at], axis=-1, keepdims=True)
        scale = c_ref[:, stream * HEAD : stream * HEAD + 1]
        e = e_ref[stream]
        probs = p_ref[stream]
        grad_image = dot_nt(gs, v[:, at])
        grad_text = dot_nt(gs, values)
        ds_image = (e.astype(f32) * ((grad_image - delta) * scale)).astype(bf16)
        ds_text = (probs.astype(f32) * (grad_text - delta)).astype(bf16)
        coef = coef_ref[stream]
        dq = dot(ds_image, k[:, at]) + dot(ds_text, keys)
        dq_ref[stream] = (dq * (coef * inv_root)).astype(bf16)
        ka_ref[stream] += dot_tn(ds_image, q[:, at])
        va_ref[stream] += dot_tn(e, (gs.astype(f32) * scale).astype(bf16))

    @pl.when(step == pl.num_programs(0) - 1)
    def _():
        for stream in range(2):
            coef = coef_ref[stream]
            dk_ref[stream] = (ka_ref[stream] * (coef * inv_root)).astype(bf16)
            dv_ref[stream] = (va_ref[stream] * coef).astype(bf16)


def backward_part(coef, qkv, ctx, e, probs, scale, attended, grads):
    S, _, tok, _ = qkv.shape
    group, steps, rows = q_blocks(S, tok)
    seq_len = S * tok
    text = ctx.shape[0]
    whole = lambda n: pl.BlockSpec((S, None, tok, LANES), lambda i: (0, n, 0, 0))
    block = pl.BlockSpec((group, tok, LANES), lambda i: (i, 0, 0))
    full = pl.BlockSpec((None, 2, seq_len, HEAD), lambda i: (0, 0, 0, 0))
    out = jax.ShapeDtypeStruct((1, 2, seq_len, HEAD), bf16)
    return pl.pallas_call(
        backward_kernel,
        grid=(steps,),
        out_shape=(out, out, out),
        in_specs=[
            smem(),
            pl.BlockSpec((group, None, tok, LANES), lambda i: (i, 0, 0, 0)),
            whole(1),
            whole(2),
            pl.BlockSpec((text, LANES), lambda i: (0, 0)),
            pl.BlockSpec((2, rows, seq_len), lambda i: (0, i, 0)),
            pl.BlockSpec((2, rows, text), lambda i: (0, i, 0)),
            pl.BlockSpec((rows, LANES), lambda i: (i, 0)),
            block,
            block,
        ],
        out_specs=(pl.BlockSpec((None, 2, rows, HEAD), lambda i: (0, 0, i, 0)), full, full),
        scratch_shapes=[pltpu.VMEM((2, seq_len, HEAD), f32)] * 2,
        compiler_params=params,
        name="backward_part",
    )(coef, qkv, qkv, qkv, ctx, e, probs, scale, attended, grads)


def exchange(x):
    return lax.all_to_all(x, "seq", split_axis=0, concat_axis=0, tiled=True)


def on_device(
    S, F, prompt, lengths, timesteps, ref_errors, gain_ffn, w_in_gate, w_in_up, w_in_down,
    gain_final, w_context, image_q, image_k, image_v, w_out, target,
):
    s = lax.axis_index("seq")
    f = lax.axis_index("fsdp")
    tok = image_q.shape[2]
    seq_len = S * tok
    qkv = exchange(pack_heads(image_q[0], image_k[0], image_v[0])).reshape(S, 3, tok, LANES)

    if F == 2 and w_in_down.shape[1] == S * LANES:
        ctx = encode_shared(
            S, prompt, lengths, gain_ffn, w_in_gate, w_in_up, w_in_down, gain_final, w_context
        )
    else:
        ctx = encode_gathered(
            prompt, gain_ffn, w_in_gate, w_in_up, w_in_down, gain_final, w_context
        )

    if F == 2:
        half = w_out.shape[0] // 2
        core = s & 1
        away = lax.dynamic_slice(w_out, (core * half, 0), (half, w_out.shape[1]))
        w_a = swap(away, "fsdp", 2, 1)
        w_b = swap(w_a, "seq", S, 1)
        weights = (w_out, w_a, w_b)
        there = 2 * (1 - f)
        w_idx = jnp.stack([2 * f, 2 * f + 1, there + core, there + 1 - core]).astype(jnp.int32)
    else:
        weights = (lax.all_gather(w_out, "fsdp", axis=0, tiled=True),)
        w_idx = jnp.arange(F, dtype=jnp.int32)

    e_img, o_img, m_img, l_img = image_part(qkv)
    attended, probs, scale = text_part(lengths, qkv, ctx, o_img, m_img, l_img)
    tokens = exchange(attended)
    grad_tok, partial_err = project(w_idx, tokens, target[0], weights)
    grads = exchange(grad_tok)
    error_sums = partial_err
    mask = 1
    while mask < S:
        error_sums = error_sums + swap(error_sums, "seq", S, mask)
        mask *= 2
    mean_errors = error_sums[:, 0] / (seq_len * target.shape[-1])
    error_gap = mean_errors[0] - ref_errors[0, 0] - (mean_errors[1] - ref_errors[0, 1])
    sigma_t = noise_level(timesteps[0])
    logit_value = dpo_beta * sigma_t * error_gap
    pair_loss = jax.nn.softplus(logit_value)[None]
    coefficient = sigma_t * jax.nn.sigmoid(logit_value)
    coef = jnp.stack([coefficient, -coefficient])
    grad_q, grad_k, grad_v = backward_part(
        coef, qkv, ctx, e_img, probs, scale, attended, grads
    )
    return pair_loss, grad_q, grad_k, grad_v


def solution(mesh):
    S, F = mesh.shape["seq"], mesh.shape["fsdp"]

    def body(*args):
        return on_device(S, F, *args)

    return jax.shard_map(
        body,
        mesh=mesh,
        in_specs=(
            P("fsdp", None, None),
            P("fsdp"),
            P("fsdp"),
            P("fsdp", None),
            P(),
            P("fsdp", "seq"),
            P("fsdp", "seq"),
            P("seq", "fsdp"),
            P(),
            P("fsdp", "seq"),
            P("fsdp", None, "seq", None),
            P("fsdp", None, "seq", None),
            P("fsdp", None, "seq", None),
            P("fsdp", None),
            P("fsdp", None, "seq", None),
        ),
        out_specs=(
            P("fsdp"),
            P("fsdp", None, None, "seq"),
            P("fsdp", None, None, "seq"),
            P("fsdp", None, None, "seq"),
        ),
        check_vma=False,
    )
```

```python
import functools
import math

import jax
import jax.numpy as jnp
from jax import lax
from jax.experimental import pallas as pl
from jax.experimental.pallas import tpu as pltpu
from jax.sharding import PartitionSpec as P


HEAD = 64
LANES = 128
CHUNKS = 2
PARTS = 3
EXTRA = 8
f32 = jnp.float32
bf16 = jnp.bfloat16

dpo_beta = 20.0
norm_eps = 1e-06
inv_root = 1.0 / math.sqrt(HEAD)


def noise_level(step_index):
    fraction = (step_index.astype(f32) + 1.0) / 1000.0
    return 3.0 * fraction / (1.0 + 2.0 * fraction)


def dot(a, b):
    return jnp.dot(a, b, preferred_element_type=f32)


def dot_nt(a, b):
    return lax.dot_general(a, b, (((1,), (1,)), ((), ())), preferred_element_type=f32)


def dot_tn(a, b):
    return lax.dot_general(a, b, (((0,), (0,)), ((), ())), preferred_element_type=f32)


def swap(x, axis, size, mask):
    return lax.ppermute(x, axis, [(i, i ^ mask) for i in range(size)])


barrier = lax.optimization_barrier


def cost(flops, *arrays, exps=0):
    moved = sum(math.prod(a.shape) * a.dtype.itemsize for a in arrays)
    return pl.CostEstimate(flops=int(flops), bytes_accessed=moved, transcendentals=int(exps))


def vmem():
    return pl.BlockSpec(memory_space=pltpu.VMEM)


def in_hbm(x):
    return pltpu.with_memory_space_constraint(x, pltpu.HBM)


def hbm():
    return pl.BlockSpec(memory_space=pltpu.HBM)


def smem():
    return pl.BlockSpec(memory_space=pltpu.SMEM)


params = pltpu.CompilerParams(vmem_limit_bytes=20 * 1024 * 1024)


def exchange(x):
    return lax.all_to_all(x, "seq", split_axis=0, concat_axis=0, tiled=True)


def pack_kernel(q_ref, k_ref, v_ref, out_ref):
    tok = q_ref.shape[1]
    for n, ref in enumerate((q_ref, k_ref, v_ref)):
        for pair in range(ref.shape[2] // LANES):
            a = ref[0, :, pair * LANES : (pair + 1) * LANES]
            b = ref[1, :, pair * LANES : (pair + 1) * LANES]
            rows = slice(n * tok, (n + 1) * tok)
            out_ref[2 * pair, rows, :] = jnp.concatenate([a[:, :HEAD], b[:, :HEAD]], axis=1)
            out_ref[2 * pair + 1, rows, :] = jnp.concatenate([a[:, HEAD:], b[:, HEAD:]], axis=1)


def pack_heads(q, k, v):
    tok, inner = q.shape[1], q.shape[2]
    return pl.pallas_call(
        pack_kernel,
        out_shape=jax.ShapeDtypeStruct((inner // HEAD, 3 * tok, LANES), bf16),
        in_specs=[vmem()] * 3,
        out_specs=vmem(),
        compiler_params=params,
        cost_estimate=cost(0, q, k, v, q, k, v),
        name="pack_heads",
    )(q, k, v)


def down_kernel(idx_ref, mine_ref, got_ref, w_ref, out_ref, wide_ref):
    units = w_ref.shape[0]
    both = mine_ref[...].astype(f32) + got_ref[...].astype(f32)
    gate = both[:, :units]
    hidden = (jax.nn.gelu(gate, approximate=True) * both[:, units:]).astype(bf16)
    wide_ref[...] = dot(hidden, w_ref[...]).astype(bf16)
    for p in range(out_ref.shape[0]):
        start = pl.multiple_of(idx_ref[p] * LANES, LANES)
        out_ref[p] = wide_ref[:, pl.ds(start, LANES)]


def down_product(idx, mine, got, w_down):
    blocks, rows = w_down.shape[1] // LANES, mine.shape[0]
    return pl.pallas_call(
        down_kernel,
        out_shape=jax.ShapeDtypeStruct((blocks, rows, LANES), bf16),
        in_specs=[smem(), vmem(), vmem(), vmem()],
        out_specs=vmem(),
        scratch_shapes=[pltpu.VMEM((rows, w_down.shape[1]), bf16)],
        compiler_params=params,
        cost_estimate=cost(2 * rows * w_down.size, mine, got, w_down, exps=mine.size // 2),
        name="down_product",
    )(idx, mine, got, w_down)


def context_kernel(idx_ref, pp_ref, gain_ref, w_ref, *refs):
    y_refs, ctx_ref, sq_ref = refs[:-2], refs[-2], refs[-1]
    rows = pp_ref.shape[0]
    acc = jnp.zeros((rows, w_ref.shape[1]), f32)
    sq = jnp.zeros((rows, LANES), f32)
    p = 0
    for ref in y_refs:
        for n in range(ref.shape[0]):
            start = pl.multiple_of(idx_ref[p] * LANES, LANES)
            state = ref[n].astype(f32) + pp_ref[:, pl.ds(start, LANES)].astype(f32)
            sq = sq + state * state
            scaled = (state * gain_ref[:, pl.ds(start, LANES)]).astype(bf16)
            acc = acc + dot(scaled, w_ref[pl.ds(start, LANES), :])
            p += 1
    ctx_ref[...] = acc.astype(bf16)
    sq_ref[...] = jnp.sum(sq.T, axis=0, keepdims=True)


def context_product(idx, packed_prompt, gain, w_context, pieces):
    rows = packed_prompt.shape[0]
    return pl.pallas_call(
        context_kernel,
        out_shape=(
            jax.ShapeDtypeStruct((rows, w_context.shape[1]), bf16),
            jax.ShapeDtypeStruct((1, rows), f32),
        ),
        in_specs=[smem()] + [vmem()] * (3 + len(pieces)),
        out_specs=(vmem(), vmem()),
        compiler_params=params,
        cost_estimate=cost(4 * rows * w_context.size, packed_prompt, w_context, *pieces),
        name="context_product",
    )(idx, packed_prompt, gain, w_context, *pieces)


def column(row):
    return jnp.broadcast_to(row, (LANES, row.shape[1])).T


def corner_kernel(at_ref, in_ref, out_ref, sem):
    rows, cols = out_ref.shape
    row = pl.multiple_of(at_ref[0] * rows, 16)
    col = pl.multiple_of(at_ref[1] * cols, LANES)
    copy = pltpu.make_async_copy(in_ref.at[pl.ds(row, rows), pl.ds(col, cols)], out_ref, sem)
    copy.start()
    copy.wait()


def corner(at, array, rows, cols):
    out = jax.ShapeDtypeStruct((rows, cols), array.dtype)
    return pl.pallas_call(
        corner_kernel,
        out_shape=out,
        in_specs=[smem(), hbm()],
        out_specs=vmem(),
        scratch_shapes=[pltpu.SemaphoreType.DMA(())],
        compiler_params=params,
        cost_estimate=cost(0, out, out),
        name="corner",
    )(at, in_hbm(array))


def weight_copies(w_refs, buf_ref, sems):
    copies = []
    rows = w_refs[0].shape[0] // CHUNKS
    for n, ref in enumerate(w_refs):
        for chunk in range(CHUNKS):
            at = pl.ds(chunk * rows, rows)
            copies.append(
                pltpu.make_async_copy(ref.at[at], buf_ref.at[n, at], sems.at[n * CHUNKS + chunk])
            )
    for copy in copies:
        copy.start()
    return copies


def two_products(normed, buf_ref, copies, out_ref):
    units = buf_ref.shape[2]
    rows = buf_ref.shape[1] // CHUNKS
    for n in range(2):
        acc = None
        for chunk in range(CHUNKS):
            copies[n * CHUNKS + chunk].wait()
            at = slice(chunk * rows, (chunk + 1) * rows)
            term = dot(normed[:, at], buf_ref[n, at, :])
            acc = term if acc is None else acc + term
        out_ref[:, n * units : (n + 1) * units] = acc.astype(bf16)


def weight_scratch(w):
    return [pltpu.VMEM((2, *w.shape), bf16), pltpu.SemaphoreType.DMA((2 * CHUNKS,))]


def gate_up_own_kernel(
    at_ref, prompt_hbm, gain_ref, wg_ref, wu_ref, out_ref, scale_ref, here_ref,
    buf_ref, sems, prompt_ref, prompt_sem,
):
    prompt_copy = pltpu.make_async_copy(prompt_hbm, prompt_ref, prompt_sem)
    prompt_copy.start()
    copies = weight_copies((wg_ref, wu_ref), buf_ref, sems)
    prompt_copy.wait()
    value = prompt_ref[...].astype(f32)
    scale = lax.rsqrt(jnp.mean(value * value, axis=-1, keepdims=True) + norm_eps)
    cols = wg_ref.shape[0]
    start = pl.multiple_of(at_ref[0] * cols, LANES)
    here_ref[...] = prompt_ref[:, pl.ds(start, cols)]
    here = here_ref[...].astype(f32)
    normed = (here * scale * gain_ref[:, pl.ds(start, cols)]).astype(bf16)
    scale_ref[...] = jnp.broadcast_to(scale, (scale.shape[0], LANES)).T[:1]
    two_products(normed, buf_ref, copies, out_ref)


def gate_up_own(at, prompt, gain, w_gate, w_up):
    rows = prompt.shape[0]
    return pl.pallas_call(
        gate_up_own_kernel,
        out_shape=(
            pltpu.HBM((rows, 2 * w_gate.shape[1]), bf16),
            jax.ShapeDtypeStruct((1, rows), f32),
            pltpu.HBM((rows, w_gate.shape[0]), bf16),
        ),
        in_specs=[smem(), hbm(), vmem(), hbm(), hbm()],
        out_specs=(vmem(), vmem(), vmem()),
        scratch_shapes=weight_scratch(w_gate)
        + [pltpu.VMEM(prompt.shape, bf16), pltpu.SemaphoreType.DMA(())],
        compiler_params=params,
        cost_estimate=cost(4 * prompt.shape[0] * w_gate.size, prompt, w_gate, w_up),
        name="gate_up_own",
    )(at, in_hbm(prompt), gain, in_hbm(w_gate), in_hbm(w_up))


def gate_up_other_kernel(
    at_ref, a_hbm, b_ref, scale_ref, gain_ref, wg_ref, wu_ref, own_hbm, select_ref, out_ref,
    parts_ref, buf_ref, sems, a_ref, own_ref, more_sems,
):
    a_copy = pltpu.make_async_copy(a_hbm, a_ref, more_sems.at[0])
    own_copy = pltpu.make_async_copy(own_hbm, own_ref, more_sems.at[1])
    a_copy.start()
    copies = weight_copies((wg_ref, wu_ref), buf_ref, sems)
    own_copy.start()
    cols = wg_ref.shape[0]
    half = a_ref.shape[0]
    rows = own_ref.shape[0]
    start = pl.multiple_of(at_ref[0] * cols, LANES)
    gain = gain_ref[:, pl.ds(start, cols)]
    scales = column(scale_ref[...])
    swapped = at_ref[1] == 1
    low, high = scales[:half, :1], scales[half:, :1]
    scale_a = jnp.where(swapped, high, low)
    scale_b = jnp.where(swapped, low, high)
    a_copy.wait()
    normed = jnp.concatenate(
        [
            (a_ref[...].astype(f32) * scale_a * gain).astype(bf16),
            (b_ref[...].astype(f32) * scale_b * gain).astype(bf16),
        ],
        axis=0,
    )
    select = select_ref[...]
    two_products(normed, buf_ref, copies, parts_ref)
    own_copy.wait()
    packed = dot(select[:, :rows], own_ref[...]) + dot(select[:, rows:], parts_ref[...])
    out_ref[...] = packed.astype(bf16)


def gate_up_other(at, a, b, scale, gain, w_gate, w_up, own, select):
    return pl.pallas_call(
        gate_up_other_kernel,
        out_shape=jax.ShapeDtypeStruct((select.shape[0], own.shape[1]), bf16),
        in_specs=[smem(), hbm()] + [vmem()] * 3 + [hbm()] * 3 + [vmem()],
        out_specs=vmem(),
        scratch_shapes=[pltpu.VMEM(own.shape, bf16)]
        + weight_scratch(w_gate)
        + [pltpu.VMEM(a.shape, bf16), pltpu.VMEM(own.shape, bf16), pltpu.SemaphoreType.DMA((2,))],
        compiler_params=params,
        cost_estimate=cost(6 * own.shape[0] * w_gate.size, a, b, w_gate, w_up, own, own),
        name="gate_up_other",
    )(at, in_hbm(a), b, scale, gain, in_hbm(w_gate), in_hbm(w_up), in_hbm(own), select)


def bit_reversed(size):
    bits = size.bit_length() - 1
    return [int(format(p, "b").zfill(bits)[::-1], 2) if bits else 0 for p in range(size)]


def encode_shared(
    S, prompt, lengths, gain_ffn, w_gate, w_up, w_down, gain_final, w_context, w_out, qkv_in
):
    s = lax.axis_index("seq")
    f = lax.axis_index("fsdp")
    own = prompt[0]
    rows, width = own.shape
    cols = width // 2
    half = rows // 2
    core = s & 1

    away = corner(jnp.stack([core, 1 - f]).astype(jnp.int32), own, half, cols)
    got_a = swap(away, "fsdp", 2, 1)
    other_len = swap(lengths, "fsdp", 2, 1)[0]
    away, own = barrier((away, own))
    at = jnp.stack([f, core]).astype(jnp.int32)
    parts_own, scale, here = gate_up_own(at, own, gain_ffn[None], w_gate, w_up)
    other_scale = swap(scale, "fsdp", 2, 1)

    first = core * half
    own_len = lengths[0]
    own_start = jnp.where(f == 0, 0, other_len)
    other_start = jnp.where(f == 0, own_len, 0)
    row = jnp.arange(half, dtype=jnp.int32)
    source = jnp.concatenate([row, row + half, row + first, row + half - first])
    is_own = jnp.arange(2 * rows) < rows
    place = source + jnp.where(is_own, own_start, other_start)
    place = jnp.where(source < jnp.where(is_own, own_len, other_len), place, -1)
    total = rows * 3 // 2
    select = (jnp.arange(total)[:, None] == place[None, :]).astype(bf16)
    got_a, parts_own, other_scale, select, here = barrier(
        (got_a, parts_own, other_scale, select, here)
    )
    got_b = swap(got_a, "seq", S, 1)

    packed = gate_up_other(
        at, got_a, got_b, other_scale, gain_ffn[None], w_gate, w_up, parts_own, select
    )
    received = swap(packed, "fsdp", 2, 1)
    packed, got_a, got_b, here, select, *qkv_in = barrier(
        (packed, got_a, got_b, here, select, *qkv_in)
    )
    blocks = pack_heads(*qkv_in)
    qkv = exchange(blocks)
    packed_prompt = dot(select, jnp.concatenate([here, got_a, got_b], axis=0)).astype(bf16)
    idx = jnp.array(bit_reversed(S), jnp.int32) ^ s
    w_half = w_out.shape[0] // 2
    w_away = corner(jnp.stack([core, 0]).astype(jnp.int32), w_out, w_half, w_out.shape[1])
    received, packed_prompt, blocks, w_away = barrier((received, packed_prompt, blocks, w_away))

    w_a = swap(w_away, "fsdp", 2, 1)

    x = down_product(idx, packed, received, w_down)

    masks = [1 << b for b in range(S.bit_length() - 1)]
    image = None
    for n, mask in enumerate(masks):
        mid = x.shape[0] // 2
        got = swap(x[mid:], "seq", S, mask)
        if n == 1:
            x, qkv = barrier((x, qkv))
            image = image_part(qkv.reshape(S, 3, -1, LANES))
            got, image = barrier((got, image))
        if n == 2:
            got, w_a = barrier((got, w_a))
            w_b = swap(w_a, "seq", S, 1)
        x = (x[:mid].astype(f32) + got.astype(f32)).astype(bf16)
    pieces = [x]
    for n, mask in enumerate(reversed(masks)):
        last = mask == 1
        if not last and len(pieces) > 1:
            pieces = [jnp.concatenate(pieces, axis=0)]
        got = [swap(piece, "seq", S, mask) for piece in pieces]
        if n == 1:
            got[0], w_b = barrier((got[0], w_b))
        pieces = pieces + got

    gain_here = lax.dynamic_slice(gain_final, (f * cols,), (cols,))[None]
    ctx, sq = context_product(idx, packed_prompt, gain_here, w_context, pieces)
    ctx_other = swap(ctx, "fsdp", 2, 1)
    sq_other = swap(sq, "fsdp", 2, 1)
    inv = lax.rsqrt((sq + sq_other)[0] / width + norm_eps)
    ctx = ((ctx.astype(f32) + ctx_other.astype(f32)) * inv[:, None]).astype(bf16)
    ctx = dot_tn(select[:, :rows], ctx).astype(bf16)
    there = 2 * (1 - f)
    w_idx = jnp.stack([2 * f, 2 * f + 1, there + core, there + 1 - core]).astype(jnp.int32)
    return ctx, qkv.reshape(S, 3, -1, LANES), image, (w_out, w_a, w_b), w_idx


def rms_gain(values, gain):
    mean_sq = jnp.mean(values * values, axis=-1, keepdims=True)
    return values * lax.rsqrt(mean_sq + norm_eps) * gain


def encode_gathered(prompt, gain_ffn, w_gate, w_up, w_down, gain_final, w_context):
    gate_full = lax.all_gather(w_gate, "fsdp", axis=0, tiled=True)
    up_full = lax.all_gather(w_up, "fsdp", axis=0, tiled=True)
    down_full = lax.all_gather(w_down, "fsdp", axis=1, tiled=True)
    context_full = lax.all_gather(w_context, "fsdp", axis=0, tiled=True)
    prompt_f32 = prompt[0].astype(f32)
    normed = rms_gain(prompt_f32, gain_ffn).astype(bf16)
    hidden = (
        jax.nn.gelu(dot(normed, gate_full), approximate=True) * dot(normed, up_full)
    ).astype(bf16)
    summed = lax.psum(dot(hidden, down_full).astype(bf16), "seq").astype(f32)
    encoded = rms_gain(prompt_f32 + summed, gain_final).astype(bf16)
    return dot(encoded, context_full).astype(bf16)


def lanes_of(stream):
    return slice(stream * HEAD, (stream + 1) * HEAD)


def rows_of(ref):
    value = ref[...]
    return value.reshape(-1, LANES)


def with_ones(values):
    return jnp.concatenate([values, jnp.ones(values.shape, values.dtype)], axis=1)


def image_kernel(q_ref, k_ref, v_ref, e_ref, o_ref, m_ref, l_ref):
    q, k, v = rows_of(q_ref), rows_of(k_ref), rows_of(v_ref)
    rows = q.shape[0]
    outs, tops, sums = [], [], []
    for stream in range(2):
        at = lanes_of(stream)
        scores = dot_nt(q[:, at] * jnp.asarray(inv_root, bf16), k[:, at])
        top = jnp.max(scores, axis=-1, keepdims=True)
        e = jnp.exp(scores - top)
        eb = e.astype(bf16)
        e_ref[stream] = eb
        both = dot(eb, with_ones(v[:, at]))
        outs.append(both[:, :HEAD])
        tops.append(jnp.broadcast_to(top, (rows, HEAD)))
        sums.append(both[:, HEAD:])
    o_ref[...] = jnp.concatenate(outs, axis=1)
    m_ref[...] = jnp.concatenate(tops, axis=1)
    l_ref[...] = jnp.concatenate(sums, axis=1)


def q_blocks(S, tok):
    rows = min(256, S * tok)
    return rows // tok, S * tok // rows, rows


def image_part(qkv):
    S, _, tok, _ = qkv.shape
    group, steps, rows = q_blocks(S, tok)
    seq_len = S * tok
    whole = lambda n: pl.BlockSpec((S, None, tok, LANES), lambda i: (0, n, 0, 0))
    flat = pl.BlockSpec((rows, LANES), lambda i: (i, 0))
    return pl.pallas_call(
        image_kernel,
        grid=(steps,),
        out_shape=(pltpu.HBM((2, seq_len, seq_len), bf16),)
        + (pltpu.HBM((seq_len, LANES), f32),) * 3,
        in_specs=[
            pl.BlockSpec((group, None, tok, LANES), lambda i: (i, 0, 0, 0)),
            whole(1),
            whole(2),
        ],
        out_specs=(pl.BlockSpec((2, rows, seq_len), lambda i: (0, i, 0)), flat, flat, flat),
        compiler_params=params,
        cost_estimate=cost(16 * seq_len * seq_len * LANES, qkv, exps=2 * seq_len * seq_len),
        name="image_part",
    )(qkv, qkv, qkv)


def text_kernel(len_ref, q_ref, ctx_ref, o_ref, m_ref, l_ref, out_ref, p_ref, c_ref):
    q = rows_of(q_ref)
    ctx = ctx_ref[...]
    keys, values = ctx[:, :HEAD], ctx[:, HEAD:]
    keep = lax.broadcasted_iota(jnp.int32, (q.shape[0], ctx.shape[0]), 1) < len_ref[0]
    outs, scales = [], []
    for stream in range(2):
        at = lanes_of(stream)
        scores = dot_nt(q[:, at] * jnp.asarray(inv_root, bf16), keys)
        scores = jnp.where(keep, scores, -jnp.inf)
        top_image = m_ref[:, stream * HEAD : stream * HEAD + 1]
        top = jnp.maximum(top_image, jnp.max(scores, axis=-1, keepdims=True))
        e = jnp.exp(scores - top)
        eb = e.astype(bf16)
        both = dot(eb, with_ones(values))
        shrink = jnp.exp(m_ref[:, at] - top)
        inv = 1.0 / (l_ref[:, at] * shrink + both[:, HEAD:])
        scale = shrink * inv
        p_ref[stream] = (e * inv[:, :1]).astype(bf16)
        outs.append(o_ref[:, at] * scale + both[:, :HEAD] * inv)
        scales.append(scale)
    out = jnp.concatenate(outs, axis=1).astype(bf16)
    out_ref[...] = out.reshape(out_ref.shape)
    c_ref[...] = jnp.concatenate(scales, axis=1)


def text_part(lengths, qkv, ctx, o_img, m_img, l_img):
    S, _, tok, _ = qkv.shape
    group, steps, rows = q_blocks(S, tok)
    seq_len = S * tok
    text = ctx.shape[0]
    flat = pl.BlockSpec((rows, LANES), lambda i: (i, 0))
    return pl.pallas_call(
        text_kernel,
        grid=(steps,),
        out_shape=(
            pltpu.HBM((S, tok, LANES), bf16),
            pltpu.HBM((2, seq_len, text), bf16),
            pltpu.HBM((seq_len, LANES), f32),
        ),
        in_specs=[
            smem(),
            pl.BlockSpec((group, None, tok, LANES), lambda i: (i, 0, 0, 0)),
            pl.BlockSpec((text, LANES), lambda i: (0, 0)),
            flat,
            flat,
            flat,
        ],
        out_specs=(
            pl.BlockSpec((group, tok, LANES), lambda i: (i, 0, 0)),
            pl.BlockSpec((2, rows, text), lambda i: (0, i, 0)),
            flat,
        ),
        compiler_params=params,
        cost_estimate=cost(
            16 * seq_len * text * LANES, o_img, m_img, l_img, exps=2 * seq_len * text
        ),
        name="text_part",
    )(lengths, qkv, ctx, in_hbm(o_img), in_hbm(m_img), in_hbm(l_img))


def project_kernel(idx_ref, o_ref, target_hbm, *refs):
    counts = len(refs) - 5
    out_ref, a_ref, target_ref, buf_ref, sems = refs[counts:]
    block_rows = a_ref.shape[2]
    copies = []
    for ref in refs[:counts]:
        for n in range(ref.shape[0] // block_rows):
            slot = len(copies)
            at = pl.ds(n * block_rows, block_rows)
            copies.append(pltpu.make_async_copy(ref.at[at], buf_ref.at[slot], sems.at[slot]))
    target_copy = pltpu.make_async_copy(target_hbm, target_ref, sems.at[len(copies)])
    for copy in (*copies, target_copy):
        copy.start()
    heads, tok = o_ref.shape[0], o_ref.shape[1]
    _, _, block_rows = a_ref.shape
    pairs = block_rows // LANES
    for pair in range(heads // 2):
        a, b = o_ref[2 * pair], o_ref[2 * pair + 1]
        at = slice((pair % pairs) * LANES, (pair % pairs + 1) * LANES)
        a_ref[pair // pairs, :tok, at] = jnp.concatenate([a[:, :HEAD], b[:, :HEAD]], axis=1)
        a_ref[pair // pairs, tok:, at] = jnp.concatenate([a[:, HEAD:], b[:, HEAD:]], axis=1)
    pred = None
    for slot, copy in enumerate(copies):
        copy.wait()
        term = dot(a_ref[idx_ref[slot]], buf_ref[slot])
        pred = term if pred is None else pred + term
    target_copy.wait()
    target = target_ref[...].reshape(2 * tok, -1).astype(f32)
    residual = pred - target
    grad = residual.astype(bf16)
    for slot in range(len(copies)):
        g = dot_nt(grad, buf_ref[slot]).astype(bf16)
        head = idx_ref[slot] * (2 * pairs)
        for pair in range(pairs):
            a = g[:tok, pair * LANES : (pair + 1) * LANES]
            b = g[tok:, pair * LANES : (pair + 1) * LANES]
            out_ref[head + 2 * pair, :tok] = jnp.concatenate([a[:, :HEAD], b[:, :HEAD]], axis=1)
            out_ref[head + 2 * pair + 1, :tok] = jnp.concatenate(
                [a[:, HEAD:], b[:, HEAD:]], axis=1
            )
    squares = residual * residual
    parts = []
    for stream in range(2):
        part = squares[stream * tok : (stream + 1) * tok]
        rest = jnp.sum(jnp.sum(part, axis=0, keepdims=True), axis=1, keepdims=True)
        rest = jnp.broadcast_to(rest, (1, LANES))
        for _ in range(PARTS):
            piece = rest.astype(bf16).astype(f32)
            parts.append(piece)
            rest = rest - piece
    row = lax.broadcasted_iota(jnp.int32, (EXTRA, LANES), 0)
    tail = jnp.zeros((EXTRA, LANES), f32)
    for n, piece in enumerate(parts):
        tail = jnp.where(row == n, piece, tail)
    tail = tail.astype(bf16)
    for head in range(heads):
        out_ref[head, tok:] = tail


def project(idx, attended, target, weights):
    S, tok, _ = attended.shape
    blocks = idx.shape[0]
    block_rows = sum(w.shape[0] for w in weights) // blocks
    return pl.pallas_call(
        project_kernel,
        out_shape=jax.ShapeDtypeStruct((S, tok + EXTRA, LANES), bf16),
        in_specs=[smem(), vmem()] + [hbm()] * (1 + len(weights)),
        out_specs=vmem(),
        scratch_shapes=[
            pltpu.VMEM((blocks, 2 * tok, block_rows), bf16),
            pltpu.VMEM(target.shape, bf16),
            pltpu.VMEM((blocks, block_rows, target.shape[-1]), bf16),
            pltpu.SemaphoreType.DMA((blocks + 1,)),
        ],
        compiler_params=params,
        cost_estimate=cost(8 * attended.size // S * S * target.shape[-1], *weights),
        name="project",
    )(idx, attended, in_hbm(target), *[in_hbm(w) for w in weights])


def dpo_terms(err_ref, step_ref, ref_ref, count):
    parts = jnp.sum(err_ref[...].astype(f32), axis=0)
    totals = [
        jnp.sum(parts[n * PARTS : (n + 1) * PARTS], axis=0, keepdims=True) for n in range(2)
    ]
    errors = jnp.concatenate(totals, axis=0) / count
    step_index = jnp.full((1, LANES), step_ref[0], jnp.int32)
    sigma_t = noise_level(step_index)
    gap = (errors[0:1] - ref_ref[0, 0]) - (errors[1:2] - ref_ref[0, 1])
    logit = dpo_beta * sigma_t * gap
    small = jnp.exp(-jnp.abs(logit))
    loss = jnp.maximum(logit, 0.0) + jnp.log1p(small)
    return loss, sigma_t * jnp.where(logit >= 0, 1.0, small) / (1.0 + small)


def backward_kernel(
    count, err_ref, step_ref, ref_ref, q_ref, k_ref, v_ref, ctx_ref, e_ref, p_ref, c_ref, o_ref, g_ref,
    loss_ref, dq_ref, dk_ref, dv_ref, ka_ref, va_ref,
):
    step = pl.program_id(0)
    loss, weight = dpo_terms(err_ref, step_ref, ref_ref, count)
    coefs = (weight[:, :1], -weight[:, :1])
    q, k, v = rows_of(q_ref), rows_of(k_ref), rows_of(v_ref)
    o, g = rows_of(o_ref), g_ref[:, : o_ref.shape[1], :].reshape(-1, LANES)
    ctx = ctx_ref[...]
    keys, values = ctx[:, :HEAD], ctx[:, HEAD:]
    products = g.astype(f32) * o.astype(f32)

    @pl.when(step == 0)
    def _():
        loss_ref[...] = loss
        ka_ref[...] = jnp.zeros_like(ka_ref)
        va_ref[...] = jnp.zeros_like(va_ref)

    dqs = []
    for stream in range(2):
        at = lanes_of(stream)
        gs = g[:, at]
        delta = jnp.sum(products[:, at], axis=-1, keepdims=True)
        scale = c_ref[:, stream * HEAD : stream * HEAD + 1]
        e = e_ref[stream]
        probs = p_ref[stream]
        grad_image = dot_nt(gs, v[:, at])
        grad_text = dot_nt(gs, values)
        ds_image = (e.astype(f32) * ((grad_image - delta) * scale)).astype(bf16)
        ds_text = (probs.astype(f32) * (grad_text - delta)).astype(bf16)
        coef = coefs[stream]
        dq = dot(ds_image, k[:, at]) + dot(ds_text, keys)
        dqs.append(dq * (coef * inv_root))
        ka_ref[stream] += dot_tn(q[:, at], ds_image)
        va_ref[stream] += dot_tn((gs.astype(f32) * scale).astype(bf16), e)
    both = jnp.concatenate(dqs, axis=1).T.astype(bf16)
    dq_ref[0] = both[:HEAD]
    dq_ref[1] = both[HEAD:]

    @pl.when(step == pl.num_programs(0) - 1)
    def _():
        for stream in range(2):
            coef = coefs[stream]
            dk_ref[stream] = (ka_ref[stream] * (coef * inv_root)).astype(bf16)
            dv_ref[stream] = (va_ref[stream] * coef).astype(bf16)


def backward_part(count, steps_in, refs_in, qkv, ctx, e, probs, scale, attended, grads):
    S, _, tok, _ = qkv.shape
    group, steps, rows = q_blocks(S, tok)
    seq_len = S * tok
    text = ctx.shape[0]
    whole = lambda n: pl.BlockSpec((S, None, tok, LANES), lambda i: (0, n, 0, 0))
    block = pl.BlockSpec((group, tok, LANES), lambda i: (i, 0, 0))
    full = pl.BlockSpec((None, 2, HEAD, seq_len), lambda i: (0, 0, 0, 0))
    out = jax.ShapeDtypeStruct((1, 2, HEAD, seq_len), bf16)
    return pl.pallas_call(
        functools.partial(backward_kernel, count),
        grid=(steps,),
        out_shape=(jax.ShapeDtypeStruct((1, LANES), f32), out, out, out),
        in_specs=[
            pl.BlockSpec((S, EXTRA, LANES), lambda i: (0, tok // EXTRA, 0)),
            smem(),
            smem(),
            pl.BlockSpec((group, None, tok, LANES), lambda i: (i, 0, 0, 0)),
            whole(1),
            whole(2),
            pl.BlockSpec((text, LANES), lambda i: (0, 0)),
            pl.BlockSpec((2, rows, seq_len), lambda i: (0, i, 0)),
            pl.BlockSpec((2, rows, text), lambda i: (0, i, 0)),
            pl.BlockSpec((rows, LANES), lambda i: (i, 0)),
            block,
            pl.BlockSpec((group, tok + EXTRA, LANES), lambda i: (i, 0, 0)),
        ],
        out_specs=(
            pl.BlockSpec((1, LANES), lambda i: (0, 0)),
            pl.BlockSpec((None, 2, HEAD, rows), lambda i: (0, 0, 0, i)),
            full,
            full,
        ),
        scratch_shapes=[pltpu.VMEM((2, HEAD, seq_len), f32)] * 2,
        compiler_params=params,
        cost_estimate=cost(40 * seq_len * seq_len * LANES, e, probs, qkv),
        name="backward_part",
    )(
        grads, steps_in, refs_in, qkv, qkv, qkv, ctx, in_hbm(e), in_hbm(probs), in_hbm(scale),
        attended, grads,
    )


def on_device(
    S, F, prompt, lengths, timesteps, ref_errors, gain_ffn, w_in_gate, w_in_up, w_in_down,
    gain_final, w_context, image_q, image_k, image_v, w_out, target,
):
    tok = image_q.shape[2]
    seq_len = S * tok
    if F == 2 and w_in_down.shape[1] == S * LANES:
        ctx, qkv, image, weights, w_idx = encode_shared(
            S, prompt, lengths, gain_ffn, w_in_gate, w_in_up, w_in_down, gain_final, w_context,
            w_out, (image_q[0], image_k[0], image_v[0]),
        )
    else:
        qkv = exchange(pack_heads(image_q[0], image_k[0], image_v[0])).reshape(S, 3, tok, LANES)
        ctx = encode_gathered(
            prompt, gain_ffn, w_in_gate, w_in_up, w_in_down, gain_final, w_context
        )
        image = image_part(qkv)
        weights = (lax.all_gather(w_out, "fsdp", axis=0, tiled=True),)
        w_idx = jnp.arange(F, dtype=jnp.int32)
    e_img, o_img, m_img, l_img = image

    attended, probs, scale = text_part(lengths, qkv, ctx, o_img, m_img, l_img)
    tokens = exchange(attended)
    grads = exchange(project(w_idx, tokens, target[0], weights))
    loss, grad_q, grad_k, grad_v = backward_part(
        seq_len * target.shape[-1], timesteps, ref_errors, qkv, ctx, e_img, probs, scale, attended,
        grads,
    )
    turn = lambda x: jnp.swapaxes(x, 2, 3)
    return loss[0, :1], turn(grad_q), turn(grad_k), turn(grad_v)


def solution(mesh):
    S, F = mesh.shape["seq"], mesh.shape["fsdp"]

    def body(*args):
        return on_device(S, F, *args)

    return jax.shard_map(
        body,
        mesh=mesh,
        in_specs=(
            P("fsdp", None, None),
            P("fsdp"),
            P("fsdp"),
            P("fsdp", None),
            P(),
            P("fsdp", "seq"),
            P("fsdp", "seq"),
            P("seq", "fsdp"),
            P(),
            P("fsdp", "seq"),
            P("fsdp", None, "seq", None),
            P("fsdp", None, "seq", None),
            P("fsdp", None, "seq", None),
            P("fsdp", None),
            P("fsdp", None, "seq", None),
        ),
        out_specs=(
            P("fsdp"),
            P("fsdp", None, None, "seq"),
            P("fsdp", None, None, "seq"),
            P("fsdp", None, None, "seq"),
        ),
        check_vma=False,
    )
```

```python
import functools
import math

import jax
import jax.numpy as jnp
from jax import lax
from jax.experimental import pallas as pl
from jax.experimental.pallas import tpu as pltpu
from jax.sharding import PartitionSpec as P


HEAD = 64
LANES = 128
CHUNKS = 2
TOKEN_CHUNKS = 2
IMAGE_PARTS = 2
PARTS = 3
EXTRA = 8
f32 = jnp.float32
bf16 = jnp.bfloat16


dpo_beta = 20.0
norm_eps = 1e-06
inv_root = 1.0 / math.sqrt(HEAD)


def noise_level(step_index):
    fraction = (step_index.astype(f32) + 1.0) / 1000.0
    return 3.0 * fraction / (1.0 + 2.0 * fraction)


def dot(a, b):
    return jnp.dot(a, b, preferred_element_type=f32)


def dot_nt(a, b):
    return lax.dot_general(a, b, (((1,), (1,)), ((), ())), preferred_element_type=f32)


def dot_tn(a, b):
    return lax.dot_general(a, b, (((0,), (0,)), ((), ())), preferred_element_type=f32)


def swap(x, axis, size, mask):
    return lax.ppermute(x, axis, [(i, i ^ mask) for i in range(size)])


barrier = lax.optimization_barrier


def cost(flops, *arrays, exps=0):
    moved = sum(math.prod(a.shape) * a.dtype.itemsize for a in arrays)
    return pl.CostEstimate(flops=int(flops), bytes_accessed=moved, transcendentals=int(exps))


def vmem():
    return pl.BlockSpec(memory_space=pltpu.VMEM)


def in_hbm(x):
    return pltpu.with_memory_space_constraint(x, pltpu.HBM)


def hbm():
    return pl.BlockSpec(memory_space=pltpu.HBM)


def smem():
    return pl.BlockSpec(memory_space=pltpu.SMEM)


params = pltpu.CompilerParams(vmem_limit_bytes=20 * 1024 * 1024)


def exchange(x):
    return lax.all_to_all(x, "seq", split_axis=0, concat_axis=0, tiled=True)


def pack_kernel(q_ref, k_ref, v_ref, out_ref):
    tok = q_ref.shape[1]
    for n, ref in enumerate((q_ref, k_ref, v_ref)):
        for pair in range(ref.shape[2] // LANES):
            a = ref[0, :, pair * LANES : (pair + 1) * LANES]
            b = ref[1, :, pair * LANES : (pair + 1) * LANES]
            rows = slice(n * tok, (n + 1) * tok)
            out_ref[2 * pair, rows, :] = jnp.concatenate([a[:, :HEAD], b[:, :HEAD]], axis=1)
            out_ref[2 * pair + 1, rows, :] = jnp.concatenate([a[:, HEAD:], b[:, HEAD:]], axis=1)


def pack_heads(q, k, v):
    tok, inner = q.shape[1], q.shape[2]
    return pl.pallas_call(
        pack_kernel,
        out_shape=jax.ShapeDtypeStruct((inner // HEAD, 3 * tok, LANES), bf16),
        in_specs=[vmem()] * 3,
        out_specs=vmem(),
        compiler_params=params,
        cost_estimate=cost(0, q, k, v, q, k, v),
        name="pack_heads",
    )(q, k, v)


def down_kernel(idx_ref, mine_ref, got_ref, w_ref, low_ref, high_ref, wide_ref):
    units = w_ref.shape[0]
    both = mine_ref[...].astype(f32) + got_ref[...].astype(f32)
    gate = both[:, :units]
    hidden = (jax.nn.gelu(gate, approximate=True) * both[:, units:]).astype(bf16)
    wide_ref[...] = dot(hidden, w_ref[...]).astype(bf16)
    blocks = low_ref.shape[0]
    for n, ref in enumerate((low_ref, high_ref)):
        for p in range(blocks):
            start = pl.multiple_of(idx_ref[n * blocks + p] * LANES, LANES)
            ref[p] = wide_ref[:, pl.ds(start, LANES)]


def down_product(idx, mine, got, w_down):
    blocks, rows = w_down.shape[1] // LANES, mine.shape[0]
    return pl.pallas_call(
        down_kernel,
        out_shape=(jax.ShapeDtypeStruct((blocks // 2, rows, LANES), bf16),) * 2,
        in_specs=[smem(), vmem(), vmem(), vmem()],
        out_specs=(vmem(), vmem()),
        scratch_shapes=[pltpu.VMEM((rows, w_down.shape[1]), bf16)],
        compiler_params=params,
        cost_estimate=cost(2 * rows * w_down.size, mine, got, w_down, exps=mine.size // 2),
        name="down_product",
    )(idx, mine, got, w_down)


def as_parts(values):
    parts = []
    for rest in values:
        for _ in range(PARTS):
            piece = rest.astype(bf16).astype(f32)
            parts.append(piece)
            rest = rest - piece
    assert len(parts) <= EXTRA
    row = lax.broadcasted_iota(jnp.int32, (EXTRA, LANES), 0)
    tail = jnp.zeros((EXTRA, LANES), f32)
    for n, piece in enumerate(parts):
        tail = jnp.where(row == n, piece, tail)
    return tail.astype(bf16)


def context_kernel(first, idx_ref, pp_ref, gain_ref, w_ref, *refs):
    y_refs, ctx_ref = refs[:-1], refs[-1]
    rows = y_refs[0].shape[1]
    acc = jnp.zeros((rows, w_ref.shape[1]), f32)
    sq = jnp.zeros((rows, LANES), f32)
    p = 0
    for ref in y_refs:
        for n in range(ref.shape[0]):
            start = pl.multiple_of(idx_ref[p] * LANES, LANES)
            base = pp_ref[first : first + rows, pl.ds(start, LANES)]
            state = ref[n].astype(f32) + base.astype(f32)
            sq = sq + state * state
            scaled = (state * gain_ref[:, pl.ds(start, LANES)]).astype(bf16)
            acc = acc + dot(scaled, w_ref[pl.ds(start, LANES), :])
            p += 1
    ctx_ref[:rows, :] = acc.astype(bf16)
    sums = jnp.sum(sq.T, axis=0, keepdims=True)
    lines = []
    for at in range(0, rows, LANES):
        line = sums[:, at : at + LANES]
        short = LANES - line.shape[1]
        if short:
            line = jnp.concatenate([line, jnp.zeros((1, short), f32)], axis=1)
        lines.append(line)
    ctx_ref[rows:, :] = as_parts(lines)


def context_product(first, idx, packed_prompt, gain, w_context, pieces):
    rows = pieces[0].shape[1]
    return pl.pallas_call(
        functools.partial(context_kernel, first),
        out_shape=jax.ShapeDtypeStruct((rows + EXTRA, w_context.shape[1]), bf16),
        in_specs=[smem()] + [vmem()] * (3 + len(pieces)),
        out_specs=vmem(),
        compiler_params=params,
        cost_estimate=cost(2 * rows * w_context.size, w_context, *pieces),
        name="context_product",
    )(idx, packed_prompt, gain, w_context, *pieces)


def finish_kernel(width, select_ref, *refs):
    out_ref = refs[-1]
    text = out_ref.shape[0]
    total = jnp.zeros(out_ref.shape, f32)
    first = 0
    for mine_ref, got_ref in zip(refs[:-1:2], refs[1:-1:2]):
        both = mine_ref[...].astype(f32) + got_ref[...].astype(f32)
        rows = both.shape[0] - EXTRA
        pieces = []
        for n, at in enumerate(range(0, rows, LANES)):
            tail = rows + n * PARTS
            sums = jnp.sum(both[tail : tail + PARTS], axis=0, keepdims=True)
            size = min(LANES, rows - at)
            inv = column(lax.rsqrt(sums / width + norm_eps))[:size]
            pieces.append((both[at : at + size] * inv).astype(bf16))
        ctx = jnp.concatenate(pieces, axis=0)
        total = total + dot_tn(select_ref[first : first + rows, :text], ctx)
        first += rows
    out_ref[...] = total.astype(bf16)


def finish_context(width, text, select, pairs):
    return pl.pallas_call(
        functools.partial(finish_kernel, width),
        out_shape=jax.ShapeDtypeStruct((text, pairs[0][0].shape[1]), bf16),
        in_specs=[vmem()] * (1 + 2 * len(pairs)),
        out_specs=vmem(),
        compiler_params=params,
        cost_estimate=cost(2 * text * select.shape[0] * LANES, select),
        name="finish_context",
    )(select, *[x for pair in pairs for x in pair])


def column(row):
    return jnp.broadcast_to(row, (LANES, row.shape[1])).T


def corner_kernel(at_ref, in_ref, out_ref, sem):
    rows, cols = out_ref.shape
    row = pl.multiple_of(at_ref[0] * rows, 16)
    col = pl.multiple_of(at_ref[1] * cols, LANES)
    copy = pltpu.make_async_copy(in_ref.at[pl.ds(row, rows), pl.ds(col, cols)], out_ref, sem)
    copy.start()
    copy.wait()


def corner(at, array, rows, cols):
    out = jax.ShapeDtypeStruct((rows, cols), array.dtype)
    return pl.pallas_call(
        corner_kernel,
        out_shape=out,
        in_specs=[smem(), hbm()],
        out_specs=vmem(),
        scratch_shapes=[pltpu.SemaphoreType.DMA(())],
        compiler_params=params,
        cost_estimate=cost(0, out, out),
        name="corner",
    )(at, in_hbm(array))


def weight_copies(w_refs, buf_ref, sems):
    copies = []
    rows = w_refs[0].shape[0] // CHUNKS
    for n, ref in enumerate(w_refs):
        for chunk in range(CHUNKS):
            at = pl.ds(chunk * rows, rows)
            copies.append(
                pltpu.make_async_copy(ref.at[at], buf_ref.at[n, at], sems.at[n * CHUNKS + chunk])
            )
    for copy in copies:
        copy.start()
    return copies


def norm_own_kernel(at_ref, prompt_ref, gain_ref, normed_ref, scale_ref):
    value = prompt_ref[...].astype(f32)
    scale = lax.rsqrt(jnp.mean(value * value, axis=-1, keepdims=True) + norm_eps)
    cols = normed_ref.shape[1]
    start = pl.multiple_of(at_ref[0] * cols, LANES)
    here = prompt_ref[:, pl.ds(start, cols)].astype(f32)
    normed_ref[...] = (here * scale * gain_ref[:, pl.ds(start, cols)]).astype(bf16)
    scale_ref[...] = jnp.broadcast_to(scale, (scale.shape[0], LANES)).T[:1]


def norm_own(at, prompt, gain, cols):
    rows = prompt.shape[0]
    return pl.pallas_call(
        norm_own_kernel,
        out_shape=(pltpu.HBM((rows, cols), bf16), jax.ShapeDtypeStruct((1, rows), f32)),
        in_specs=[smem(), vmem(), vmem()],
        out_specs=(vmem(), vmem()),
        compiler_params=params,
        cost_estimate=cost(0, prompt, prompt),
        name="norm_own",
    )(at, prompt, gain)


def gate_up_kernel(
    at_ref, a_hbm, b_ref, scale_ref, gain_ref, wg_ref, wu_ref, own_hbm, select_ref, *refs
):
    out_refs = refs[:-5]
    normed_ref, parts_ref, buf_ref, sems, a_ref = refs[-5:]
    half, cols = a_ref.shape
    rows = 2 * half
    a_copy = pltpu.make_async_copy(a_hbm, a_ref, sems.at[2 * CHUNKS])
    own_copy = pltpu.make_async_copy(own_hbm, normed_ref.at[pl.ds(0, rows)], sems.at[2 * CHUNKS + 1])
    a_copy.start()
    own_copy.start()
    copies = weight_copies((wg_ref, wu_ref), buf_ref, sems)
    start = pl.multiple_of(at_ref[0] * cols, LANES)
    gain = gain_ref[:, pl.ds(start, cols)]
    scales = column(scale_ref[...])
    swapped = at_ref[1] == 1
    low, high = scales[:half, :1], scales[half:, :1]
    scale_a = jnp.where(swapped, high, low)
    scale_b = jnp.where(swapped, low, high)
    normed_ref[rows + half :, :] = (b_ref[...].astype(f32) * scale_b * gain).astype(bf16)
    a_copy.wait()
    normed_ref[rows : rows + half, :] = (a_ref[...].astype(f32) * scale_a * gain).astype(bf16)
    own_copy.wait()
    units = buf_ref.shape[2]
    depth = cols // CHUNKS
    for n in range(2):
        acc = None
        for chunk in range(CHUNKS):
            copies[n * CHUNKS + chunk].wait()
            part = slice(chunk * depth, (chunk + 1) * depth)
            term = dot(normed_ref[:, part], buf_ref[n, part, :])
            acc = term if acc is None else acc + term
        parts_ref[:, n * units : (n + 1) * units] = acc.astype(bf16)
    for chunk, out_ref in enumerate(out_refs):
        size = out_ref.shape[0]
        select = select_ref[chunk * size : (chunk + 1) * size, :]
        out_ref[...] = dot(select, parts_ref[...]).astype(bf16)


def gate_up(at, a, b, scale, gain, w_gate, w_up, own, select):
    total, rows = select.shape
    cols, units = w_gate.shape
    size = total // TOKEN_CHUNKS
    return pl.pallas_call(
        gate_up_kernel,
        out_shape=(jax.ShapeDtypeStruct((size, 2 * units), bf16),) * TOKEN_CHUNKS,
        in_specs=[smem(), hbm()] + [vmem()] * 3 + [hbm()] * 3 + [vmem()],
        out_specs=(vmem(),) * TOKEN_CHUNKS,
        scratch_shapes=[
            pltpu.VMEM((rows, cols), bf16),
            pltpu.VMEM((rows, 2 * units), bf16),
            pltpu.VMEM((2, cols, units), bf16),
            pltpu.SemaphoreType.DMA((2 * CHUNKS + 2,)),
            pltpu.VMEM(a.shape, bf16),
        ],
        compiler_params=params,
        cost_estimate=cost(4 * rows * w_gate.size, a, b, w_gate, w_up, own),
        name="gate_up",
    )(at, in_hbm(a), b, scale, gain, in_hbm(w_gate), in_hbm(w_up), in_hbm(own), select)


def pack_rows_kernel(at_ref, prompt_hbm, a_ref, b_ref, select_ref, out_ref, rows_ref, sem):
    half, cols = a_ref.shape
    rows = 2 * half
    start = pl.multiple_of(at_ref[0] * cols, LANES)
    copy = pltpu.make_async_copy(
        prompt_hbm.at[:, pl.ds(start, cols)], rows_ref.at[pl.ds(0, rows)], sem
    )
    copy.start()
    rows_ref[rows : rows + half, :] = a_ref[...]
    rows_ref[rows + half :, :] = b_ref[...]
    copy.wait()
    out_ref[...] = dot(select_ref[...], rows_ref[...]).astype(bf16)


def pack_rows(at, prompt, a, b, select):
    cols = a.shape[1]
    return pl.pallas_call(
        pack_rows_kernel,
        out_shape=jax.ShapeDtypeStruct((select.shape[0], cols), bf16),
        in_specs=[smem(), hbm(), vmem(), vmem(), vmem()],
        out_specs=vmem(),
        scratch_shapes=[pltpu.VMEM((select.shape[1], cols), bf16), pltpu.SemaphoreType.DMA(())],
        compiler_params=params,
        cost_estimate=cost(2 * select.size * cols, a, b, a, b, a, b),
        name="pack_rows",
    )(at, in_hbm(prompt), a, b, select)


def encode_shared(
    S, prompt, lengths, gain_ffn, w_gate, w_up, w_down, gain_final, w_context, w_out, qkv_in
):
    s = lax.axis_index("seq")
    f = lax.axis_index("fsdp")
    own = prompt[0]
    rows, width = own.shape
    cols = width // 2
    half = rows // 2
    core = s & 1

    away = corner(jnp.stack([core, 1 - f]).astype(jnp.int32), own, half, cols)
    got_a = swap(away, "fsdp", 2, 1)
    other_len = swap(lengths, "fsdp", 2, 1)[0]
    away, own = barrier((away, own))
    at = jnp.stack([f, core]).astype(jnp.int32)
    normed_own, scale = norm_own(at, own, gain_ffn[None], cols)
    other_scale = swap(scale, "fsdp", 2, 1)
    normed_own, *qkv_in = barrier((normed_own, *qkv_in))
    blocks = pack_heads(*qkv_in)
    qkv = exchange(blocks)
    qkv = qkv.reshape(S, 3, -1, LANES)

    first = core * half
    own_len = lengths[0]
    own_start = jnp.where(f == 0, 0, other_len)
    other_start = jnp.where(f == 0, own_len, 0)
    row = jnp.arange(half, dtype=jnp.int32)
    source = jnp.concatenate([row, row + half, row + first, row + half - first])
    is_own = jnp.arange(2 * rows) < rows
    place = source + jnp.where(is_own, own_start, other_start)
    place = jnp.where(source < jnp.where(is_own, own_len, other_len), place, -1)
    total = rows * 3 // 2
    select = (jnp.arange(total)[:, None] == place[None, :]).astype(bf16)
    got_a, other_scale, select = barrier((got_a, other_scale, select))
    got_b = swap(got_a, "seq", S, 1)

    packed = gate_up(
        at, got_a, got_b, other_scale, gain_ffn[None], w_gate, w_up, normed_own, select
    )
    received = []
    for part in packed:
        received.append(swap(part, "fsdp", 2, 1))
    first_part, got_a, got_b = barrier((packed[0], got_a, got_b))
    packed = [first_part, *packed[1:]]
    packed_prompt = pack_rows(at, own, got_a, got_b, select)
    received[0], packed_prompt = barrier((received[0], packed_prompt))
    w_half = w_out.shape[0] // 2
    w_away = corner(jnp.stack([core, 0]).astype(jnp.int32), w_out, w_half, w_out.shape[1])
    w_a = swap(w_away, "fsdp", 2, 1)
    w_b = swap(w_a, "seq", S, 1)

    rest = S // 4
    order = [c + 2 * x + 4 * j for c in range(2) for x in range(2) for j in range(rest)]
    idx = jnp.array(order, jnp.int32) ^ s
    gain_here = lax.dynamic_slice(gain_final, (f * cols,), (cols,))[None]
    add = lambda *terms: sum(t.astype(f32) for t in terms).astype(bf16)
    pairs = []
    image = None
    for c in range(TOKEN_CHUNKS):

        def move(value, mask):
            return swap(value, "seq", S, mask)

        low, high = down_product(idx, packed[c], received[c], w_down)
        got = move(high, 1)
        send = add(low[rest:], got[rest:])
        got_x = move(send, 2)
        keep = add(low[:rest], got[:rest])
        mine = [add(keep[j : j + 1], got_x[j : j + 1]) for j in range(rest)]
        got_z = [move(mine[j], 4 * j) for j in range(1, rest)]
        block = add(mine[0], *got_z)
        near = [block] + [move(block, 4 * j) for j in range(1, rest)]
        near = jnp.concatenate(near, axis=0)
        far = move(near, 2)
        pieces = [near, far, move(near, 1), move(far, 1)]
        size = packed[c].shape[0]
        ctx = context_product(c * size, idx, packed_prompt, gain_here, w_context, pieces)
        pairs.append((ctx, swap(ctx, "fsdp", 2, 1)))
    for part in range(IMAGE_PARTS):
        image = image_part(qkv, part, IMAGE_PARTS, image)
    ctx = finish_context(width, rows, select, pairs)
    there = 2 * (1 - f)
    w_idx = jnp.stack([2 * f, 2 * f + 1, there + core, there + 1 - core]).astype(jnp.int32)
    return ctx, qkv, image, (w_out, w_a, w_b), w_idx


def rms_gain(values, gain):
    mean_sq = jnp.mean(values * values, axis=-1, keepdims=True)
    return values * lax.rsqrt(mean_sq + norm_eps) * gain


def encode_gathered(prompt, gain_ffn, w_gate, w_up, w_down, gain_final, w_context):
    gate_full = lax.all_gather(w_gate, "fsdp", axis=0, tiled=True)
    up_full = lax.all_gather(w_up, "fsdp", axis=0, tiled=True)
    down_full = lax.all_gather(w_down, "fsdp", axis=1, tiled=True)
    context_full = lax.all_gather(w_context, "fsdp", axis=0, tiled=True)
    prompt_f32 = prompt[0].astype(f32)
    normed = rms_gain(prompt_f32, gain_ffn).astype(bf16)
    hidden = (
        jax.nn.gelu(dot(normed, gate_full), approximate=True) * dot(normed, up_full)
    ).astype(bf16)
    summed = lax.psum(dot(hidden, down_full).astype(bf16), "seq").astype(f32)
    encoded = rms_gain(prompt_f32 + summed, gain_final).astype(bf16)
    return dot(encoded, context_full).astype(bf16)


def rows_of(ref):
    value = ref[...]
    return value.reshape(-1, LANES)


def first_lanes(x):
    return lax.broadcasted_iota(jnp.int32, x.shape, 1) < HEAD


def by_stream(first, second):
    return jnp.where(first_lanes(first), first, second)


def wide(first, second):
    shape = (first.shape[0], LANES)
    return by_stream(jnp.broadcast_to(first, shape), jnp.broadcast_to(second, shape))


def masked(x):
    none = jnp.zeros_like(x)
    return by_stream(x, none), by_stream(none, x)


def turned(x):
    return jnp.concatenate([x[:, HEAD:], x[:, :HEAD]], axis=1)


def with_sums(values):
    ones = masked(jnp.ones(values[0].shape, bf16))
    return [jnp.concatenate([v, one], axis=1) for v, one in zip(values, ones)]


def image_kernel(q_ref, k_ref, v_ref, *refs):
    e_ref, o_ref, m_ref, l_ref = refs[-4:]
    q = rows_of(q_ref) * jnp.asarray(inv_root, bf16)
    keys = masked(rows_of(k_ref))
    values = with_sums(masked(rows_of(v_ref)))
    both, tops = None, []
    for stream in range(2):
        scores = dot_nt(q, keys[stream])
        top = jnp.max(scores, axis=-1, keepdims=True)
        e = jnp.exp(scores - top).astype(bf16)
        e_ref[stream] = e
        term = dot(e, values[stream])
        both = term if both is None else both + term
        tops.append(top)
    o_ref[...] = both[:, :LANES]
    l_ref[...] = both[:, LANES:]
    m_ref[...] = wide(*tops)


def q_blocks(S, tok):
    rows = min(256, S * tok)
    return rows // tok, S * tok // rows, rows


def image_part(qkv, part, parts, previous=None):
    S, _, tok, _ = qkv.shape
    group, steps, rows = q_blocks(S, tok)
    seq_len = S * tok
    steps //= parts
    first = part * steps
    whole = lambda n: pl.BlockSpec((S, None, tok, LANES), lambda i: (0, n, 0, 0))
    flat = pl.BlockSpec((rows, LANES), lambda i: (first + i, 0))
    earlier = () if previous is None else previous
    return pl.pallas_call(
        image_kernel,
        grid=(steps,),
        out_shape=(pltpu.HBM((2, seq_len, seq_len), bf16),)
        + (pltpu.HBM((seq_len, LANES), f32),) * 3,
        in_specs=[
            pl.BlockSpec((group, None, tok, LANES), lambda i: (first + i, 0, 0, 0)),
            whole(1),
            whole(2),
        ]
        + [pl.BlockSpec(memory_space=pltpu.HBM)] * len(earlier),
        out_specs=(
            pl.BlockSpec((2, rows, seq_len), lambda i: (0, first + i, 0)), flat, flat, flat,
        ),
        input_output_aliases={3 + n: n for n in range(len(earlier))},
        compiler_params=params,
        cost_estimate=cost(
            16 * seq_len * seq_len * LANES // parts, qkv, exps=2 * seq_len * seq_len // parts
        ),
        name="image_part",
    )(qkv, qkv, qkv, *earlier)


def text_sides(ctx):
    other = turned(ctx)
    none = jnp.zeros_like(ctx)
    keys = (by_stream(ctx, none), by_stream(none, other))
    return keys, (by_stream(other, none), by_stream(none, ctx))


def text_kernel(len_ref, q_ref, ctx_ref, o_ref, m_ref, l_ref, out_ref, e_ref, ci_ref, ct_ref):
    q = rows_of(q_ref) * jnp.asarray(inv_root, bf16)
    keys, values = text_sides(ctx_ref[...])
    values = with_sums(values)
    keep = lax.broadcasted_iota(jnp.int32, (q.shape[0], ctx_ref.shape[0]), 1) < len_ref[0]
    both, tops = None, []
    for stream in range(2):
        scores = jnp.where(keep, dot_nt(q, keys[stream]), -jnp.inf)
        top = jnp.max(scores, axis=-1, keepdims=True)
        e = jnp.exp(scores - top).astype(bf16)
        e_ref[stream] = e
        term = dot(e, values[stream])
        both = term if both is None else both + term
        tops.append(top)
    top_text = wide(*tops)
    top_image = m_ref[...]
    top = jnp.maximum(top_image, top_text)
    shrink_image = jnp.exp(top_image - top)
    shrink_text = jnp.exp(top_text - top)
    inv = 1.0 / (l_ref[...] * shrink_image + both[:, LANES:] * shrink_text)
    scale_image = shrink_image * inv
    scale_text = shrink_text * inv
    out = o_ref[...] * scale_image + both[:, :LANES] * scale_text
    out_ref[...] = out.astype(bf16).reshape(out_ref.shape)
    ci_ref[...] = scale_image
    ct_ref[...] = scale_text


def text_part(lengths, qkv, ctx, o_img, m_img, l_img):
    S, _, tok, _ = qkv.shape
    group, steps, rows = q_blocks(S, tok)
    seq_len = S * tok
    text = ctx.shape[0]
    flat = pl.BlockSpec((rows, LANES), lambda i: (i, 0))
    return pl.pallas_call(
        text_kernel,
        grid=(steps,),
        out_shape=(
            pltpu.HBM((S, tok, LANES), bf16),
            pltpu.HBM((2, seq_len, text), bf16),
            pltpu.HBM((seq_len, LANES), f32),
            pltpu.HBM((seq_len, LANES), f32),
        ),
        in_specs=[
            smem(),
            pl.BlockSpec((group, None, tok, LANES), lambda i: (i, 0, 0, 0)),
            pl.BlockSpec((text, LANES), lambda i: (0, 0)),
            flat,
            flat,
            flat,
        ],
        out_specs=(
            pl.BlockSpec((group, tok, LANES), lambda i: (i, 0, 0)),
            pl.BlockSpec((2, rows, text), lambda i: (0, i, 0)),
            flat,
            flat,
        ),
        compiler_params=params,
        cost_estimate=cost(16 * seq_len * ctx.size, o_img, m_img, l_img, exps=2 * seq_len * text),
        name="text_part",
    )(lengths, qkv, ctx, in_hbm(o_img), in_hbm(m_img), in_hbm(l_img))


def load_kernel(target_hbm, *refs):
    counts = len(refs) - 3
    target_ref, buf_ref, sems = refs[counts:]
    block_rows = buf_ref.shape[1]
    copies = [pltpu.make_async_copy(target_hbm, target_ref, sems.at[0])]
    for ref in refs[:counts]:
        for n in range(ref.shape[0] // block_rows):
            slot = len(copies)
            at = pl.ds(n * block_rows, block_rows)
            copies.append(pltpu.make_async_copy(ref.at[at], buf_ref.at[slot - 1], sems.at[slot]))
    for copy in copies:
        copy.start()
    for copy in copies:
        copy.wait()


def load_weights(blocks, target, weights):
    rows = sum(w.shape[0] for w in weights) // blocks
    return pl.pallas_call(
        load_kernel,
        out_shape=(
            jax.ShapeDtypeStruct(target.shape, bf16),
            jax.ShapeDtypeStruct((blocks, rows, target.shape[-1]), bf16),
        ),
        in_specs=[hbm()] * (1 + len(weights)),
        out_specs=(vmem(), vmem()),
        scratch_shapes=[pltpu.SemaphoreType.DMA((blocks + 1,))],
        compiler_params=params,
        cost_estimate=cost(0, target, target, *weights, *weights),
        name="load_weights",
    )(in_hbm(target), *[in_hbm(w) for w in weights])


def project_kernel(idx_ref, o_ref, target_ref, w_ref, out_ref, a_ref):
    heads, tok = o_ref.shape[0], o_ref.shape[1]
    blocks, _, block_rows = a_ref.shape
    pairs = block_rows // LANES
    for pair in range(heads // 2):
        a, b = o_ref[2 * pair], o_ref[2 * pair + 1]
        at = slice((pair % pairs) * LANES, (pair % pairs + 1) * LANES)
        a_ref[pair // pairs, :tok, at] = jnp.concatenate([a[:, :HEAD], b[:, :HEAD]], axis=1)
        a_ref[pair // pairs, tok:, at] = jnp.concatenate([a[:, HEAD:], b[:, HEAD:]], axis=1)
    pred = None
    for slot in range(blocks):
        term = dot(a_ref[idx_ref[slot]], w_ref[slot])
        pred = term if pred is None else pred + term
    target = target_ref[...].reshape(2 * tok, -1).astype(f32)
    residual = pred - target
    grad = residual.astype(bf16)
    for slot in range(blocks):
        g = dot_nt(grad, w_ref[slot]).astype(bf16)
        head = idx_ref[slot] * (2 * pairs)
        for pair in range(pairs):
            a = g[:tok, pair * LANES : (pair + 1) * LANES]
            b = g[tok:, pair * LANES : (pair + 1) * LANES]
            out_ref[head + 2 * pair, :tok] = jnp.concatenate([a[:, :HEAD], b[:, :HEAD]], axis=1)
            out_ref[head + 2 * pair + 1, :tok] = jnp.concatenate(
                [a[:, HEAD:], b[:, HEAD:]], axis=1
            )
    squares = residual * residual
    totals = []
    for stream in range(2):
        part = squares[stream * tok : (stream + 1) * tok]
        total = jnp.sum(jnp.sum(part, axis=0, keepdims=True), axis=1, keepdims=True)
        totals.append(jnp.broadcast_to(total, (1, LANES)))
    tail = as_parts(totals)
    for head in range(heads):
        out_ref[head, tok:] = tail


def project(idx, attended, target, weights):
    S, tok, _ = attended.shape
    blocks, block_rows, _ = weights.shape
    return pl.pallas_call(
        project_kernel,
        out_shape=jax.ShapeDtypeStruct((S, tok + EXTRA, LANES), bf16),
        in_specs=[smem()] + [vmem()] * 3,
        out_specs=vmem(),
        scratch_shapes=[pltpu.VMEM((blocks, 2 * tok, block_rows), bf16)],
        compiler_params=params,
        cost_estimate=cost(8 * tok * weights.size, weights, attended, attended, target),
        name="project",
    )(idx, attended, target, weights)


def dpo_terms(err_ref, step_ref, ref_ref, count):
    parts = jnp.sum(err_ref[...].astype(f32), axis=0)
    totals = [
        jnp.sum(parts[n * PARTS : (n + 1) * PARTS], axis=0, keepdims=True) for n in range(2)
    ]
    errors = jnp.concatenate(totals, axis=0) / count
    step_index = jnp.full((1, LANES), step_ref[0], jnp.int32)
    sigma_t = noise_level(step_index)
    gap = (errors[0:1] - ref_ref[0, 0]) - (errors[1:2] - ref_ref[0, 1])
    logit = dpo_beta * sigma_t * gap
    small = jnp.exp(-jnp.abs(logit))
    loss = jnp.maximum(logit, 0.0) + jnp.log1p(small)
    return loss, sigma_t * jnp.where(logit >= 0, 1.0, small) / (1.0 + small)


def lane_in_half(x):
    return lax.broadcasted_iota(jnp.int32, x.shape, 1) % HEAD


def score_grads(g, delta, scale, values, weights):
    scaled = (g * scale).astype(bf16)
    term = -(delta * scale)
    term = jnp.concatenate([term[:, HEAD:], term[:, :HEAD]], axis=1)
    high = term.astype(bf16).astype(f32)
    place = lane_in_half(term)
    extra = jnp.where(place == 0, high, jnp.where(place == 1, term - high, 0.0)).astype(bf16)
    left = (by_stream(scaled, extra), by_stream(extra, scaled))
    grads = []
    for stream in range(2):
        product = dot_nt(left[stream], values[stream])
        grads.append((weights[stream].astype(f32) * product).astype(bf16))
    return grads, scaled


def with_marks(values):
    marks = (lane_in_half(values[0]) < 2).astype(bf16)
    return by_stream(values[0], marks), by_stream(marks, values[1])


def backward_kernel(
    count, err_ref, step_ref, ref_ref, q_ref, k_ref, v_ref, ctx_ref, e_ref, p_ref, ci_ref, ct_ref,
    o_ref, g_ref, loss_ref, dq_ref, dk_ref, dv_ref, ka_ref, va_ref,
):
    step = pl.program_id(0)
    loss, weight = dpo_terms(err_ref, step_ref, ref_ref, count)
    q = rows_of(q_ref)
    keys = masked(rows_of(k_ref))
    values = with_marks(masked(rows_of(v_ref)))
    text_keys, text_values = text_sides(ctx_ref[...])
    text_values = with_marks(text_values)
    o = rows_of(o_ref).astype(f32)
    g = g_ref[:, : o_ref.shape[1], :].reshape(-1, LANES).astype(f32)

    @pl.when(step == 0)
    def _():
        loss_ref[...] = loss
        ka_ref[...] = jnp.zeros_like(ka_ref)
        va_ref[...] = jnp.zeros_like(va_ref)

    delta = wide(*[jnp.sum(part, axis=-1, keepdims=True) for part in masked(g * o)])
    e = [e_ref[0], e_ref[1]]
    image, scaled = score_grads(g, delta, ci_ref[...], values, e)
    text, _ = score_grads(g, delta, ct_ref[...], text_values, [p_ref[0], p_ref[1]])
    dq = None
    for stream in range(2):
        term = dot(image[stream], keys[stream]) + dot(text[stream], text_keys[stream])
        dq = term if dq is None else dq + term
        at = slice(stream * HEAD, (stream + 1) * HEAD)
        ka_ref[stream] += dot_tn(q, image[stream])[at]
        va_ref[stream] += dot_tn(scaled, e[stream])[at]
    signed = wide(weight[:, :1], -weight[:, :1])
    turned_dq = (dq * (signed * inv_root)).T.astype(bf16)
    dq_ref[0] = turned_dq[:HEAD]
    dq_ref[1] = turned_dq[HEAD:]

    @pl.when(step == pl.num_programs(0) - 1)
    def _():
        for stream, coef in enumerate((weight[:, :1], -weight[:, :1])):
            dk_ref[stream] = (ka_ref[stream] * (coef * inv_root)).astype(bf16)
            dv_ref[stream] = (va_ref[stream] * coef).astype(bf16)


def backward_part(count, steps_in, refs_in, qkv, ctx, e, e_text, scales, attended, grads):
    S, _, tok, _ = qkv.shape
    group, steps, rows = q_blocks(S, tok)
    seq_len = S * tok
    text = ctx.shape[0]
    whole = lambda n: pl.BlockSpec((S, None, tok, LANES), lambda i: (0, n, 0, 0))
    block = pl.BlockSpec((group, tok, LANES), lambda i: (i, 0, 0))
    full = pl.BlockSpec((None, 2, HEAD, seq_len), lambda i: (0, 0, 0, 0))
    out = jax.ShapeDtypeStruct((1, 2, HEAD, seq_len), bf16)
    return pl.pallas_call(
        functools.partial(backward_kernel, count),
        grid=(steps,),
        out_shape=(jax.ShapeDtypeStruct((1, LANES), f32), out, out, out),
        in_specs=[
            pl.BlockSpec((S, EXTRA, LANES), lambda i: (0, tok // EXTRA, 0)),
            smem(),
            smem(),
            pl.BlockSpec((group, None, tok, LANES), lambda i: (i, 0, 0, 0)),
            whole(1),
            whole(2),
            pl.BlockSpec((text, LANES), lambda i: (0, 0)),
            pl.BlockSpec((2, rows, seq_len), lambda i: (0, i, 0)),
            pl.BlockSpec((2, rows, text), lambda i: (0, i, 0)),
            pl.BlockSpec((rows, LANES), lambda i: (i, 0)),
            pl.BlockSpec((rows, LANES), lambda i: (i, 0)),
            block,
            pl.BlockSpec((group, tok + EXTRA, LANES), lambda i: (i, 0, 0)),
        ],
        out_specs=(
            pl.BlockSpec((1, LANES), lambda i: (0, 0)),
            pl.BlockSpec((None, 2, HEAD, rows), lambda i: (0, 0, 0, i)),
            full,
            full,
        ),
        scratch_shapes=[pltpu.VMEM((2, HEAD, seq_len), f32)] * 2,
        compiler_params=params,
        cost_estimate=cost(40 * seq_len * seq_len * LANES, e, e_text, qkv),
        name="backward_part",
    )(
        grads, steps_in, refs_in, qkv, qkv, qkv, ctx, in_hbm(e), in_hbm(e_text),
        *[in_hbm(x) for x in scales], attended, grads,
    )


def on_device(
    S, F, prompt, lengths, timesteps, ref_errors, gain_ffn, w_in_gate, w_in_up, w_in_down,
    gain_final, w_context, image_q, image_k, image_v, w_out, target,
):
    tok = image_q.shape[2]
    seq_len = S * tok
    if F == 2 and w_in_down.shape[1] == S * LANES:
        ctx, qkv, image, weights, w_idx = encode_shared(
            S, prompt, lengths, gain_ffn, w_in_gate, w_in_up, w_in_down, gain_final, w_context,
            w_out, (image_q[0], image_k[0], image_v[0]),
        )
    else:
        qkv = exchange(pack_heads(image_q[0], image_k[0], image_v[0])).reshape(S, 3, tok, LANES)
        ctx = encode_gathered(
            prompt, gain_ffn, w_in_gate, w_in_up, w_in_down, gain_final, w_context
        )
        image = image_part(qkv, 0, 1)
        weights = (lax.all_gather(w_out, "fsdp", axis=0, tiled=True),)
        w_idx = jnp.arange(F, dtype=jnp.int32)
    e_img, o_img, m_img, l_img = image

    attended, e_text, *scales = text_part(lengths, qkv, ctx, o_img, m_img, l_img)
    tokens = exchange(attended)
    loaded, blocks = load_weights(w_idx.shape[0], target[0], weights)
    grads = exchange(project(w_idx, tokens, loaded, blocks))
    loss, grad_q, grad_k, grad_v = backward_part(
        seq_len * target.shape[-1], timesteps, ref_errors, qkv, ctx, e_img, e_text, scales,
        attended, grads,
    )
    turn = lambda x: jnp.swapaxes(x, 2, 3)
    return loss[0, :1], turn(grad_q), turn(grad_k), turn(grad_v)


def solution(mesh):
    S, F = mesh.shape["seq"], mesh.shape["fsdp"]

    def body(*args):
        return on_device(S, F, *args)

    return jax.shard_map(
        body,
        mesh=mesh,
        in_specs=(
            P("fsdp", None, None),
            P("fsdp"),
            P("fsdp"),
            P("fsdp", None),
            P(),
            P("fsdp", "seq"),
            P("fsdp", "seq"),
            P("seq", "fsdp"),
            P(),
            P("fsdp", "seq"),
            P("fsdp", None, "seq", None),
            P("fsdp", None, "seq", None),
            P("fsdp", None, "seq", None),
            P("fsdp", None),
            P("fsdp", None, "seq", None),
        ),
        out_specs=(
            P("fsdp"),
            P("fsdp", None, None, "seq"),
            P("fsdp", None, None, "seq"),
            P("fsdp", None, None, "seq"),
        ),
        check_vma=False,
    )
```

```python
import functools
import math

import jax
import jax.numpy as jnp
from jax import lax
from jax.experimental import pallas as pl
from jax.experimental.pallas import tpu as pltpu
from jax.sharding import PartitionSpec as P


HEAD = 64
LANES = 128
FIRST_SHARE = 8
IMAGE_PARTS = 2
PARTS = 3
EXTRA = 8
f32 = jnp.float32
bf16 = jnp.bfloat16


dpo_beta = 20.0
norm_eps = 1e-06
inv_root = 1.0 / math.sqrt(HEAD)


def noise_level(step_index):
    fraction = (step_index.astype(f32) + 1.0) / 1000.0
    return 3.0 * fraction / (1.0 + 2.0 * fraction)


def dot(a, b):
    return jnp.dot(a, b, preferred_element_type=f32)


def dot_nt(a, b):
    return lax.dot_general(a, b, (((1,), (1,)), ((), ())), preferred_element_type=f32)


def dot_tn(a, b):
    return lax.dot_general(a, b, (((0,), (0,)), ((), ())), preferred_element_type=f32)


def swap(x, axis, size, mask):
    return lax.ppermute(x, axis, [(i, i ^ mask) for i in range(size)])


barrier = lax.optimization_barrier


def cost(flops, *arrays, exps=0):
    moved = sum(math.prod(a.shape) * a.dtype.itemsize for a in arrays)
    return pl.CostEstimate(flops=int(flops), bytes_accessed=moved, transcendentals=int(exps))


def vmem():
    return pl.BlockSpec(memory_space=pltpu.VMEM)


def in_hbm(x):
    return pltpu.with_memory_space_constraint(x, pltpu.HBM)


def hbm():
    return pl.BlockSpec(memory_space=pltpu.HBM)


def smem():
    return pl.BlockSpec(memory_space=pltpu.SMEM)


params = pltpu.CompilerParams(vmem_limit_bytes=20 * 1024 * 1024)


def exchange(x):
    return lax.all_to_all(x, "seq", split_axis=0, concat_axis=0, tiled=True)


def pack_kernel(q_ref, k_ref, v_ref, out_ref):
    tok = q_ref.shape[1]
    for n, ref in enumerate((q_ref, k_ref, v_ref)):
        for pair in range(ref.shape[2] // LANES):
            a = ref[0, :, pair * LANES : (pair + 1) * LANES]
            b = ref[1, :, pair * LANES : (pair + 1) * LANES]
            rows = slice(n * tok, (n + 1) * tok)
            out_ref[2 * pair, rows, :] = jnp.concatenate([a[:, :HEAD], b[:, :HEAD]], axis=1)
            out_ref[2 * pair + 1, rows, :] = jnp.concatenate([a[:, HEAD:], b[:, HEAD:]], axis=1)


def pack_heads(q, k, v):
    tok, inner = q.shape[1], q.shape[2]
    return pl.pallas_call(
        pack_kernel,
        out_shape=jax.ShapeDtypeStruct((inner // HEAD, 3 * tok, LANES), bf16),
        in_specs=[vmem()] * 3,
        out_specs=vmem(),
        compiler_params=params,
        cost_estimate=cost(0, q, k, v, q, k, v),
        name="pack_heads",
    )(q, k, v)


def down_half(side, at_ref, idx_ref, hidden, w_ref, out_ref, wide_ref):
    blocks = out_ref.shape[0]
    width = blocks * LANES
    half = at_ref[1] if side == 0 else 1 - at_ref[1]
    base = half * width
    start = pl.multiple_of(base, LANES)
    wide_ref[...] = dot(hidden, w_ref[:, pl.ds(start, width)]).astype(bf16)
    for p in range(blocks):
        start = pl.multiple_of(idx_ref[side * blocks + p] * LANES - base, LANES)
        out_ref[p] = wide_ref[:, pl.ds(start, LANES)]


def down_away_kernel(at_ref, idx_ref, mine_ref, got_ref, w_ref, out_ref, hidden_ref, wide_ref):
    units = w_ref.shape[0]
    both = mine_ref[...].astype(f32) + got_ref[...].astype(f32)
    gate = both[:, :units]
    hidden = (jax.nn.gelu(gate, approximate=True) * both[:, units:]).astype(bf16)
    hidden_ref[...] = hidden
    down_half(1, at_ref, idx_ref, hidden, w_ref, out_ref, wide_ref)


def down_stay_kernel(at_ref, idx_ref, hidden_ref, w_ref, out_ref, wide_ref):
    down_half(0, at_ref, idx_ref, hidden_ref[...], w_ref, out_ref, wide_ref)


def down_product(side, at, idx, w_down, *rows_in):
    blocks, rows = w_down.shape[1] // LANES // 2, rows_in[0].shape[0]
    out = jax.ShapeDtypeStruct((blocks, rows, LANES), bf16)
    hidden = jax.ShapeDtypeStruct((rows, w_down.shape[0]), bf16)
    return pl.pallas_call(
        down_away_kernel if side else down_stay_kernel,
        out_shape=(out, hidden) if side else out,
        in_specs=[smem(), smem()] + [vmem()] * (len(rows_in) + 1),
        out_specs=(vmem(), vmem()) if side else vmem(),
        scratch_shapes=[pltpu.VMEM((rows, blocks * LANES), bf16)],
        compiler_params=params,
        cost_estimate=cost(rows * w_down.size, out, hidden, w_down, exps=hidden.size),
        name="down_product",
    )(at, idx, *rows_in, w_down)


def as_parts(values):
    parts = []
    for rest in values:
        for _ in range(PARTS):
            piece = rest.astype(bf16).astype(f32)
            parts.append(piece)
            rest = rest - piece
    assert len(parts) <= EXTRA
    row = lax.broadcasted_iota(jnp.int32, (EXTRA, LANES), 0)
    tail = jnp.zeros((EXTRA, LANES), f32)
    for n, piece in enumerate(parts):
        tail = jnp.where(row == n, piece, tail)
    return tail.astype(bf16)


def context_kernel(first, at_ref, idx_ref, pp_ref, gain_ref, w_ref, *refs):
    y_refs, ctx_ref = refs[:-1], refs[-1]
    rows = y_refs[0].shape[1]
    acc = jnp.zeros((rows, w_ref.shape[1]), f32)
    sq = jnp.zeros((rows, LANES), f32)
    p = 0
    for ref in y_refs:
        for n in range(ref.shape[0]):
            start = pl.multiple_of(idx_ref[p] * LANES, LANES)
            base = pp_ref[first : first + rows, pl.ds(start, LANES)]
            state = ref[n].astype(f32) + base.astype(f32)
            sq = sq + state * state
            there = pl.multiple_of(at_ref[0] * pp_ref.shape[1] + start, LANES)
            scaled = (state * gain_ref[:, pl.ds(there, LANES)]).astype(bf16)
            acc = acc + dot(scaled, w_ref[pl.ds(start, LANES), :])
            p += 1
    ctx_ref[:rows, :] = acc.astype(bf16)
    sums = jnp.sum(sq.T, axis=0, keepdims=True)
    lines = []
    for at in range(0, rows, LANES):
        line = sums[:, at : at + LANES]
        short = LANES - line.shape[1]
        if short:
            line = jnp.concatenate([line, jnp.zeros((1, short), f32)], axis=1)
        lines.append(line)
    ctx_ref[rows:, :] = as_parts(lines)


def context_product(first, at, idx, packed_prompt, gain, w_context, pieces):
    rows = pieces[0].shape[1]
    return pl.pallas_call(
        functools.partial(context_kernel, first),
        out_shape=jax.ShapeDtypeStruct((rows + EXTRA, w_context.shape[1]), bf16),
        in_specs=[smem(), smem()] + [vmem()] * (3 + len(pieces)),
        out_specs=vmem(),
        compiler_params=params,
        cost_estimate=cost(2 * rows * w_context.size, w_context, *pieces),
        name="context_product",
    )(at, idx, packed_prompt, gain, w_context, *pieces)


def finish_kernel(width, select_ref, *refs):
    out_ref = refs[-1]
    text = out_ref.shape[0]
    total = jnp.zeros(out_ref.shape, f32)
    first = 0
    for mine_ref, got_ref in zip(refs[:-1:2], refs[1:-1:2]):
        both = mine_ref[...].astype(f32) + got_ref[...].astype(f32)
        rows = both.shape[0] - EXTRA
        pieces = []
        for n, at in enumerate(range(0, rows, LANES)):
            tail = rows + n * PARTS
            sums = jnp.sum(both[tail : tail + PARTS], axis=0, keepdims=True)
            size = min(LANES, rows - at)
            inv = column(lax.rsqrt(sums / width + norm_eps))[:size]
            pieces.append((both[at : at + size] * inv).astype(bf16))
        ctx = jnp.concatenate(pieces, axis=0)
        total = total + dot_tn(select_ref[first : first + rows, :text], ctx)
        first += rows
    out_ref[...] = total.astype(bf16)


def finish_context(width, text, select, pairs):
    return pl.pallas_call(
        functools.partial(finish_kernel, width),
        out_shape=jax.ShapeDtypeStruct((text, pairs[0][0].shape[1]), bf16),
        in_specs=[vmem()] * (1 + 2 * len(pairs)),
        out_specs=vmem(),
        compiler_params=params,
        cost_estimate=cost(2 * text * select.shape[0] * LANES, select),
        name="finish_context",
    )(select, *[x for pair in pairs for x in pair])


def column(row):
    return jnp.broadcast_to(row, (LANES, row.shape[1])).T


def corner_kernel(row_at, col_at, at_ref, in_ref, out_ref, sem):
    rows, cols = out_ref.shape
    row = pl.multiple_of(at_ref[row_at] * rows, 16)
    col = 0 if col_at is None else pl.multiple_of(at_ref[col_at] * cols, LANES)
    copy = pltpu.make_async_copy(in_ref.at[pl.ds(row, rows), pl.ds(col, cols)], out_ref, sem)
    copy.start()
    copy.wait()


def corner(at, array, rows, cols, row_at, col_at):
    out = jax.ShapeDtypeStruct((rows, cols), array.dtype)
    return pl.pallas_call(
        functools.partial(corner_kernel, row_at, col_at),
        out_shape=out,
        in_specs=[smem(), hbm()],
        out_specs=vmem(),
        scratch_shapes=[pltpu.SemaphoreType.DMA(())],
        compiler_params=params,
        cost_estimate=cost(0, out, out),
        name="corner",
    )(at, in_hbm(array))


def fetch_kernel(in_ref, out_ref, sem):
    copy = pltpu.make_async_copy(in_ref, out_ref, sem)
    copy.start()
    copy.wait()


def fetch(array):
    out = jax.ShapeDtypeStruct(array.shape, array.dtype)
    return pl.pallas_call(
        fetch_kernel,
        out_shape=out,
        in_specs=[hbm()],
        out_specs=vmem(),
        scratch_shapes=[pltpu.SemaphoreType.DMA(())],
        compiler_params=params,
        cost_estimate=cost(0, out, out),
        name="fetch",
    )(in_hbm(array))


def norm_own_kernel(at_ref, prompt_hbm, gain_ref, normed_ref, scale_ref, prompt_ref, sem):
    copy = pltpu.make_async_copy(prompt_hbm, prompt_ref, sem)
    copy.start()
    copy.wait()
    value = prompt_ref[...].astype(f32)
    scale = lax.rsqrt(jnp.mean(value * value, axis=-1, keepdims=True) + norm_eps)
    cols = normed_ref.shape[1]
    start = pl.multiple_of(at_ref[0] * cols, LANES)
    here = prompt_ref[:, pl.ds(start, cols)].astype(f32)
    normed_ref[...] = (here * scale * gain_ref[:, pl.ds(start, cols)]).astype(bf16)
    scale_ref[...] = jnp.broadcast_to(scale, (scale.shape[0], LANES)).T[:1]


def norm_own(at, prompt, gain, cols):
    rows = prompt.shape[0]
    return pl.pallas_call(
        norm_own_kernel,
        out_shape=(
            jax.ShapeDtypeStruct((rows, cols), bf16), jax.ShapeDtypeStruct((1, rows), f32),
        ),
        in_specs=[smem(), hbm(), vmem()],
        out_specs=(vmem(), vmem()),
        scratch_shapes=[pltpu.VMEM(prompt.shape, bf16), pltpu.SemaphoreType.DMA(())],
        compiler_params=params,
        cost_estimate=cost(0, prompt, prompt),
        name="norm_own",
    )(at, in_hbm(prompt), gain)


def packed_places(at_ref, own_len, other_len, shape):
    _, count = shape
    rows = count // 2
    half = rows // 2
    f, core = at_ref[0], at_ref[1]
    column_at = lax.broadcasted_iota(jnp.int32, shape, 1)
    is_own = column_at < rows
    got = column_at - rows + core * half
    got = jnp.where(got >= rows, got - rows, got)
    source = jnp.where(is_own, column_at, got)
    limit = jnp.where(is_own, own_len, other_len)
    start = jnp.where(is_own, f * other_len, (1 - f) * own_len)
    hit = lax.broadcasted_iota(jnp.int32, shape, 0) == source + start
    return jnp.where(hit & (source < limit), 1.0, 0.0).astype(bf16)


def packed_product(select, own, other, gate, out_ref):
    rows, units = own.shape[0], gate.shape[1]
    packed = dot(select[:, :rows], own[...]) + dot(select[:, rows:], other[...])
    packed = packed.astype(bf16)
    out_ref[:, :units] = dot(packed, gate[...]).astype(bf16)
    return packed


def gate_up_first_kernel(
    at_ref, own_len_ref, other_len_ref, a_ref, b_ref, scale_ref, gain_ref, gate_ref, up_hbm,
    own_ref, select_ref, out_ref, normed_ref, up_ref, sem,
):
    copy = pltpu.make_async_copy(up_hbm, up_ref, sem)
    copy.start()
    half, cols = a_ref.shape
    start = pl.multiple_of(at_ref[0] * cols, LANES)
    gain = gain_ref[:, pl.ds(start, cols)]
    scales = column(scale_ref[...])
    swapped = at_ref[1] == 1
    low, high = scales[:half, :1], scales[half:, :1]
    scale_a = jnp.where(swapped, high, low)
    scale_b = jnp.where(swapped, low, high)
    normed_ref[:half, :] = (a_ref[...].astype(f32) * scale_a * gain).astype(bf16)
    normed_ref[half:, :] = (b_ref[...].astype(f32) * scale_b * gain).astype(bf16)
    select_ref[...] = packed_places(at_ref, own_len_ref[0], other_len_ref[0], select_ref.shape)
    size, units = out_ref.shape[0], gate_ref.shape[1]
    packed = packed_product(select_ref[:size, :], own_ref, normed_ref, gate_ref, out_ref)
    copy.wait()
    out_ref[:, units:] = dot(packed, up_ref[...]).astype(bf16)


def gate_up_first(size, at, own_len, other_len, a, b, scale, gain, gate, w_up, own, total):
    shape = lambda *dims: jax.ShapeDtypeStruct(dims, bf16)
    return pl.pallas_call(
        gate_up_first_kernel,
        out_shape=(
            shape(total, 2 * own.shape[0]), shape(size, 2 * w_up.shape[1]), shape(*own.shape),
            shape(*w_up.shape),
        ),
        in_specs=[smem()] * 3 + [vmem()] * 5 + [hbm(), vmem()],
        out_specs=(vmem(),) * 4,
        scratch_shapes=[pltpu.SemaphoreType.DMA(())],
        compiler_params=params,
        cost_estimate=cost(6 * size * w_up.size, a, b, gate, w_up, own),
        name="gate_up_first",
    )(at, own_len, other_len, a, b, scale, gain, gate, in_hbm(w_up), own)


def gate_up_next_kernel(first, select_ref, own_ref, other_ref, gate_ref, up_ref, out_ref):
    size, units = out_ref.shape[0], gate_ref.shape[1]
    select = select_ref[first : first + size, :]
    packed = packed_product(select, own_ref, other_ref, gate_ref, out_ref)
    out_ref[:, units:] = dot(packed, up_ref[...]).astype(bf16)


def gate_up_next(first, size, select, own, other, gate, up):
    return pl.pallas_call(
        functools.partial(gate_up_next_kernel, first),
        out_shape=jax.ShapeDtypeStruct((size, 2 * up.shape[1]), bf16),
        in_specs=[vmem()] * 5,
        out_specs=vmem(),
        compiler_params=params,
        cost_estimate=cost(6 * size * up.size, select, own, other, gate, up),
        name="gate_up_next",
    )(select, own, other, gate, up)


def pack_rows_kernel(at_ref, prompt_hbm, a_ref, b_ref, select_ref, out_ref, rows_ref, sem):
    half, cols = a_ref.shape
    rows = 2 * half
    start = pl.multiple_of(at_ref[0] * cols, LANES)
    copy = pltpu.make_async_copy(
        prompt_hbm.at[:, pl.ds(start, cols)], rows_ref.at[pl.ds(0, rows)], sem
    )
    copy.start()
    rows_ref[rows : rows + half, :] = a_ref[...]
    rows_ref[rows + half :, :] = b_ref[...]
    copy.wait()
    out_ref[...] = dot(select_ref[...], rows_ref[...]).astype(bf16)


def pack_rows(at, prompt, a, b, select):
    cols = a.shape[1]
    return pl.pallas_call(
        pack_rows_kernel,
        out_shape=jax.ShapeDtypeStruct((select.shape[0], cols), bf16),
        in_specs=[smem(), hbm(), vmem(), vmem(), vmem()],
        out_specs=vmem(),
        scratch_shapes=[pltpu.VMEM((select.shape[1], cols), bf16), pltpu.SemaphoreType.DMA(())],
        compiler_params=params,
        cost_estimate=cost(2 * select.size * cols, a, b, a, b, a, b),
        name="pack_rows",
    )(at, in_hbm(prompt), a, b, select)


def chunk_sizes(total):
    first = total * FIRST_SHARE // 16 // 16 * 16
    return first, total - first


def encode_shared(
    S, prompt, lengths, gain_ffn, w_gate, w_up, w_down, gain_final, w_context, w_out, qkv_in
):
    s = lax.axis_index("seq")
    f = lax.axis_index("fsdp")
    own = prompt[0]
    rows, width = own.shape
    cols = width // 2
    half = rows // 2
    core = s & 1

    there = 2 * (1 - f)
    at = jnp.stack(
        [f, core, 1 - f, 2 * f, 2 * f + 1, there + core, there + 1 - core]
    ).astype(jnp.int32)
    rest = S // 4
    place = core * (S // 2) + (s >> 1 & 1) * rest + (s >> 2)
    idx = jnp.arange(S, dtype=jnp.int32) ^ place
    away = corner(at, own, half, cols, 1, 2)
    got_a = swap(away, "fsdp", 2, 1)
    other_len = swap(lengths, "fsdp", 2, 1)
    away, own, at, idx, *qkv_in = barrier((away, own, at, idx, *qkv_in))
    blocks = pack_heads(*qkv_in)
    qkv = exchange(blocks)
    qkv = qkv.reshape(S, 3, -1, LANES)
    normed_own, scale = norm_own(at, own, gain_ffn[None], cols)
    other_scale = swap(scale, "fsdp", 2, 1)

    total = rows * 3 // 2
    got_a, other_scale, other_len = barrier((got_a, other_scale, other_len))
    got_b = swap(got_a, "seq", S, 1)
    gate = fetch(w_gate)

    sizes = chunk_sizes(total)
    select, part, normed_other, up = gate_up_first(
        sizes[0], at, lengths, other_len, got_a, got_b, other_scale, gain_ffn[None], gate, w_up,
        normed_own, total,
    )
    packed, received, first = [], [], 0
    for c, size in enumerate(sizes):
        if c:
            part = gate_up_next(first, size, select, normed_own, normed_other, gate, up)
        packed.append(part)
        received.append(swap(part, "fsdp", 2, 1))
        first += size
    first_part, got_a, got_b = barrier((packed[0], got_a, got_b))
    packed = [first_part, *packed[1:]]
    packed_prompt = pack_rows(at, own, got_a, got_b, select)
    received[0], packed_prompt = barrier((received[0], packed_prompt))
    w_half = w_out.shape[0] // 2
    w_away = corner(at, w_out, w_half, w_out.shape[1], 1, None)
    w_a = swap(w_away, "fsdp", 2, 1)
    w_b = swap(w_a, "seq", S, 1)

    add = lambda *terms: sum(t.astype(f32) for t in terms).astype(bf16)
    pairs = []
    image = None
    first = 0
    for c, size in enumerate(sizes):

        def move(value, mask):
            return swap(value, "seq", S, mask)

        high, hidden = down_product(1, at, idx, w_down, packed[c], received[c])
        got = move(high, 1)
        low = down_product(0, at, idx, w_down, hidden)
        got_half = move(add(low[rest:], got[rest:]), 2)
        mine = [add(low[j : j + 1], got[j : j + 1], got_half[j : j + 1]) for j in range(rest)]
        near = add(mine[0], *[move(mine[j], 4 * j) for j in range(1, rest)])
        near = [near] + [move(near, 4 * j) for j in range(1, rest)]
        near = jnp.concatenate(near, axis=0)
        far = move(near, 2)
        pieces = [near, far, move(near, 1), move(far, 1)]
        ctx = context_product(first, at, idx, packed_prompt, gain_final[None], w_context, pieces)
        pairs.append((ctx, swap(ctx, "fsdp", 2, 1)))
        first += size
    for part in range(IMAGE_PARTS):
        image = image_part(qkv, part, IMAGE_PARTS, image)
    ctx = finish_context(width, rows, select, pairs)
    ctx, w_b = barrier((ctx, w_b))
    return ctx, qkv, image, (w_out, w_a, w_b), at


def rms_gain(values, gain):
    mean_sq = jnp.mean(values * values, axis=-1, keepdims=True)
    return values * lax.rsqrt(mean_sq + norm_eps) * gain


def encode_gathered(prompt, gain_ffn, w_gate, w_up, w_down, gain_final, w_context):
    gate_full = lax.all_gather(w_gate, "fsdp", axis=0, tiled=True)
    up_full = lax.all_gather(w_up, "fsdp", axis=0, tiled=True)
    down_full = lax.all_gather(w_down, "fsdp", axis=1, tiled=True)
    context_full = lax.all_gather(w_context, "fsdp", axis=0, tiled=True)
    prompt_f32 = prompt[0].astype(f32)
    normed = rms_gain(prompt_f32, gain_ffn).astype(bf16)
    hidden = (
        jax.nn.gelu(dot(normed, gate_full), approximate=True) * dot(normed, up_full)
    ).astype(bf16)
    summed = lax.psum(dot(hidden, down_full).astype(bf16), "seq").astype(f32)
    encoded = rms_gain(prompt_f32 + summed, gain_final).astype(bf16)
    return dot(encoded, context_full).astype(bf16)


def rows_of(ref):
    value = ref[...]
    return value.reshape(-1, LANES)


def first_lanes(x):
    return lax.broadcasted_iota(jnp.int32, x.shape, 1) < HEAD


def by_stream(first, second):
    return jnp.where(first_lanes(first), first, second)


def wide(first, second):
    shape = (first.shape[0], LANES)
    return by_stream(jnp.broadcast_to(first, shape), jnp.broadcast_to(second, shape))


def masked(x):
    none = jnp.zeros_like(x)
    return by_stream(x, none), by_stream(none, x)


def turned(x):
    return jnp.concatenate([x[:, HEAD:], x[:, :HEAD]], axis=1)


def with_sums(values):
    ones = masked(jnp.ones(values[0].shape, bf16))
    return [jnp.concatenate([v, one], axis=1) for v, one in zip(values, ones)]


def image_kernel(q_ref, k_ref, v_ref, *refs):
    e_ref, o_ref, m_ref, l_ref = refs[-4:]
    q = rows_of(q_ref) * jnp.asarray(inv_root, bf16)
    keys = masked(rows_of(k_ref))
    values = with_sums(masked(rows_of(v_ref)))
    both, tops = None, []
    for stream in range(2):
        scores = dot_nt(q, keys[stream])
        top = jnp.max(scores, axis=-1, keepdims=True)
        e = jnp.exp(scores - top).astype(bf16)
        e_ref[stream] = e
        term = dot(e, values[stream])
        both = term if both is None else both + term
        tops.append(top)
    o_ref[...] = both[:, :LANES]
    l_ref[...] = both[:, LANES:]
    m_ref[...] = wide(*tops)


def q_blocks(S, tok, rows=256):
    rows = min(rows, S * tok)
    return rows // tok, S * tok // rows, rows


def image_part(qkv, part, parts, previous=None):
    S, _, tok, _ = qkv.shape
    group, steps, rows = q_blocks(S, tok, 512)
    seq_len = S * tok
    steps //= parts
    first = part * steps
    whole = lambda n: pl.BlockSpec((S, None, tok, LANES), lambda i: (0, n, 0, 0))
    flat = pl.BlockSpec((rows, LANES), lambda i: (first + i, 0))
    earlier = () if previous is None else previous
    return pl.pallas_call(
        image_kernel,
        grid=(steps,),
        out_shape=(pltpu.HBM((2, seq_len, seq_len), bf16),)
        + (jax.ShapeDtypeStruct((seq_len, LANES), f32),) * 3,
        in_specs=[
            pl.BlockSpec((group, None, tok, LANES), lambda i: (first + i, 0, 0, 0)),
            whole(1),
            whole(2),
        ]
        + [pl.BlockSpec(memory_space=pl.ANY)] * len(earlier),
        out_specs=(
            pl.BlockSpec((2, rows, seq_len), lambda i: (0, first + i, 0)), flat, flat, flat,
        ),
        input_output_aliases={3 + n: n for n in range(len(earlier))},
        compiler_params=params,
        cost_estimate=cost(
            16 * seq_len * seq_len * LANES // parts, qkv, exps=2 * seq_len * seq_len // parts
        ),
        name="image_part",
    )(qkv, qkv, qkv, *earlier)


def text_sides(ctx):
    other = turned(ctx)
    none = jnp.zeros_like(ctx)
    keys = (by_stream(ctx, none), by_stream(none, other))
    return keys, (by_stream(other, none), by_stream(none, ctx))


def text_kernel(len_ref, q_ref, ctx_ref, o_ref, m_ref, l_ref, out_ref, e_ref, ci_ref, ct_ref):
    q = rows_of(q_ref) * jnp.asarray(inv_root, bf16)
    keys, values = text_sides(ctx_ref[...])
    values = with_sums(values)
    keep = lax.broadcasted_iota(jnp.int32, (q.shape[0], ctx_ref.shape[0]), 1) < len_ref[0]
    both, tops = None, []
    for stream in range(2):
        scores = jnp.where(keep, dot_nt(q, keys[stream]), -jnp.inf)
        top = jnp.max(scores, axis=-1, keepdims=True)
        e = jnp.exp(scores - top).astype(bf16)
        e_ref[stream] = e
        term = dot(e, values[stream])
        both = term if both is None else both + term
        tops.append(top)
    top_text = wide(*tops)
    top_image = m_ref[...]
    top = jnp.maximum(top_image, top_text)
    shrink_image = jnp.exp(top_image - top)
    shrink_text = jnp.exp(top_text - top)
    inv = 1.0 / (l_ref[...] * shrink_image + both[:, LANES:] * shrink_text)
    scale_image = shrink_image * inv
    scale_text = shrink_text * inv
    out = o_ref[...] * scale_image + both[:, :LANES] * scale_text
    out_ref[...] = out.astype(bf16).reshape(out_ref.shape)
    ci_ref[...] = scale_image
    ct_ref[...] = scale_text


def text_part(lengths, qkv, ctx, o_img, m_img, l_img):
    S, _, tok, _ = qkv.shape
    group, steps, rows = q_blocks(S, tok, 512)
    seq_len = S * tok
    text = ctx.shape[0]
    flat = pl.BlockSpec((rows, LANES), lambda i: (i, 0))
    return pl.pallas_call(
        text_kernel,
        grid=(steps,),
        out_shape=(
            pltpu.HBM((S, tok, LANES), bf16),
            pltpu.HBM((2, seq_len, text), bf16),
            pltpu.HBM((seq_len, LANES), f32),
            pltpu.HBM((seq_len, LANES), f32),
        ),
        in_specs=[
            smem(),
            pl.BlockSpec((group, None, tok, LANES), lambda i: (i, 0, 0, 0)),
            pl.BlockSpec((text, LANES), lambda i: (0, 0)),
            flat,
            flat,
            flat,
        ],
        out_specs=(
            pl.BlockSpec((group, tok, LANES), lambda i: (i, 0, 0)),
            pl.BlockSpec((2, rows, text), lambda i: (0, i, 0)),
            flat,
            flat,
        ),
        compiler_params=params,
        cost_estimate=cost(16 * seq_len * ctx.size, o_img, m_img, l_img, exps=2 * seq_len * text),
        name="text_part",
    )(lengths, qkv, ctx, o_img, m_img, l_img)


def project_kernel(first, idx_ref, o_ref, target_hbm, *refs):
    counts = len(refs) - 5
    out_ref, a_ref, target_ref, w_ref, sems = refs[counts:]
    block_rows = w_ref.shape[1]
    copies = []
    for ref in refs[:counts]:
        for n in range(ref.shape[0] // block_rows):
            slot = len(copies)
            rows = pl.ds(n * block_rows, block_rows)
            copies.append(pltpu.make_async_copy(ref.at[rows], w_ref.at[slot], sems.at[slot]))
    target_copy = pltpu.make_async_copy(target_hbm, target_ref, sems.at[len(copies)])
    for copy in (*copies, target_copy):
        copy.start()
    heads, tok = o_ref.shape[0], o_ref.shape[1]
    blocks, _, block_rows = a_ref.shape
    pairs = block_rows // LANES
    for pair in range(heads // 2):
        a, b = o_ref[2 * pair], o_ref[2 * pair + 1]
        at = slice((pair % pairs) * LANES, (pair % pairs + 1) * LANES)
        a_ref[pair // pairs, :tok, at] = jnp.concatenate([a[:, :HEAD], b[:, :HEAD]], axis=1)
        a_ref[pair // pairs, tok:, at] = jnp.concatenate([a[:, HEAD:], b[:, HEAD:]], axis=1)
    pred = None
    for slot, copy in enumerate(copies):
        copy.wait()
        term = dot(a_ref[idx_ref[first + slot]], w_ref[slot])
        pred = term if pred is None else pred + term
    target_copy.wait()
    target = target_ref[...].reshape(2 * tok, -1).astype(f32)
    residual = pred - target
    grad = residual.astype(bf16)
    for slot in range(blocks):
        g = dot_nt(grad, w_ref[slot]).astype(bf16)
        head = idx_ref[first + slot] * (2 * pairs)
        for pair in range(pairs):
            a = g[:tok, pair * LANES : (pair + 1) * LANES]
            b = g[tok:, pair * LANES : (pair + 1) * LANES]
            out_ref[head + 2 * pair, :tok] = jnp.concatenate([a[:, :HEAD], b[:, :HEAD]], axis=1)
            out_ref[head + 2 * pair + 1, :tok] = jnp.concatenate(
                [a[:, HEAD:], b[:, HEAD:]], axis=1
            )
    squares = residual * residual
    totals = []
    for stream in range(2):
        part = squares[stream * tok : (stream + 1) * tok]
        total = jnp.sum(jnp.sum(part, axis=0, keepdims=True), axis=1, keepdims=True)
        totals.append(jnp.broadcast_to(total, (1, LANES)))
    tail = as_parts(totals)
    for head in range(heads):
        out_ref[head, tok:] = tail


def project(first, idx, attended, target, weights):
    S, tok, _ = attended.shape
    blocks = idx.shape[0] - first
    rows = sum(w.shape[0] for w in weights) // blocks
    width = target.shape[-1]
    return pl.pallas_call(
        functools.partial(project_kernel, first),
        out_shape=jax.ShapeDtypeStruct((S, tok + EXTRA, LANES), bf16),
        in_specs=[smem(), vmem()] + [hbm()] * (1 + len(weights)),
        out_specs=vmem(),
        scratch_shapes=[
            pltpu.VMEM((blocks, 2 * tok, rows), bf16),
            pltpu.VMEM(target.shape, bf16),
            pltpu.VMEM((blocks, rows, width), bf16),
            pltpu.SemaphoreType.DMA((blocks + 1,)),
        ],
        compiler_params=params,
        cost_estimate=cost(8 * tok * blocks * rows * width, *weights, attended, attended, target),
        name="project",
    )(idx, attended, in_hbm(target), *[in_hbm(w) for w in weights])


def dpo_terms(err_ref, step_ref, ref_ref, count):
    parts = jnp.sum(err_ref[...].astype(f32), axis=0)
    totals = [
        jnp.sum(parts[n * PARTS : (n + 1) * PARTS], axis=0, keepdims=True) for n in range(2)
    ]
    errors = jnp.concatenate(totals, axis=0) / count
    step_index = jnp.full((1, LANES), step_ref[0], jnp.int32)
    sigma_t = noise_level(step_index)
    gap = (errors[0:1] - ref_ref[0, 0]) - (errors[1:2] - ref_ref[0, 1])
    logit = dpo_beta * sigma_t * gap
    small = jnp.exp(-jnp.abs(logit))
    loss = jnp.maximum(logit, 0.0) + jnp.log1p(small)
    return loss, sigma_t * jnp.where(logit >= 0, 1.0, small) / (1.0 + small)


def lane_in_half(x):
    return lax.broadcasted_iota(jnp.int32, x.shape, 1) % HEAD


def score_grads(g, delta, scale, values, weights):
    scaled = (g * scale).astype(bf16)
    term = -(delta * scale)
    term = jnp.concatenate([term[:, HEAD:], term[:, :HEAD]], axis=1)
    high = term.astype(bf16).astype(f32)
    place = lane_in_half(term)
    extra = jnp.where(place == 0, high, jnp.where(place == 1, term - high, 0.0)).astype(bf16)
    left = (by_stream(scaled, extra), by_stream(extra, scaled))
    grads = []
    for stream in range(2):
        product = dot_nt(left[stream], values[stream])
        grads.append((weights[stream].astype(f32) * product).astype(bf16))
    return grads, scaled


def with_marks(values):
    marks = (lane_in_half(values[0]) < 2).astype(bf16)
    return by_stream(values[0], marks), by_stream(marks, values[1])


def backward_kernel(
    count, err_ref, step_ref, ref_ref, q_ref, k_ref, v_ref, ctx_ref, e_ref, p_ref, ci_ref, ct_ref,
    o_ref, g_ref, loss_ref, dq_ref, dk_ref, dv_ref, ka_ref, va_ref,
):
    step = pl.program_id(0)
    loss, weight = dpo_terms(err_ref, step_ref, ref_ref, count)
    q = rows_of(q_ref)
    keys = masked(rows_of(k_ref))
    values = with_marks(masked(rows_of(v_ref)))
    text_keys, text_values = text_sides(ctx_ref[...])
    text_values = with_marks(text_values)
    o = rows_of(o_ref).astype(f32)
    g = g_ref[:, : o_ref.shape[1], :].reshape(-1, LANES).astype(f32)

    @pl.when(step == 0)
    def _():
        loss_ref[...] = loss
        ka_ref[...] = jnp.zeros_like(ka_ref)
        va_ref[...] = jnp.zeros_like(va_ref)

    delta = wide(*[jnp.sum(part, axis=-1, keepdims=True) for part in masked(g * o)])
    e = [e_ref[0], e_ref[1]]
    image, scaled = score_grads(g, delta, ci_ref[...], values, e)
    text, _ = score_grads(g, delta, ct_ref[...], text_values, [p_ref[0], p_ref[1]])
    dq = None
    for stream in range(2):
        term = dot(image[stream], keys[stream]) + dot(text[stream], text_keys[stream])
        dq = term if dq is None else dq + term
        at = slice(stream * HEAD, (stream + 1) * HEAD)
        ka_ref[stream] += dot_tn(q, image[stream])[at]
        va_ref[stream] += dot_tn(scaled, e[stream])[at]
    signed = wide(weight[:, :1], -weight[:, :1])
    turned_dq = (dq * (signed * inv_root)).T.astype(bf16)
    dq_ref[0] = turned_dq[:HEAD]
    dq_ref[1] = turned_dq[HEAD:]

    @pl.when(step == pl.num_programs(0) - 1)
    def _():
        for stream, coef in enumerate((weight[:, :1], -weight[:, :1])):
            dk_ref[stream] = (ka_ref[stream] * (coef * inv_root)).astype(bf16)
            dv_ref[stream] = (va_ref[stream] * coef).astype(bf16)


def backward_part(count, steps_in, refs_in, qkv, ctx, e, e_text, scales, attended, grads):
    S, _, tok, _ = qkv.shape
    group, steps, rows = q_blocks(S, tok)
    seq_len = S * tok
    text = ctx.shape[0]
    whole = lambda n: pl.BlockSpec((S, None, tok, LANES), lambda i: (0, n, 0, 0))
    block = pl.BlockSpec((group, tok, LANES), lambda i: (i, 0, 0))
    full = pl.BlockSpec((None, 2, HEAD, seq_len), lambda i: (0, 0, 0, 0))
    out = jax.ShapeDtypeStruct((1, 2, HEAD, seq_len), bf16)
    return pl.pallas_call(
        functools.partial(backward_kernel, count),
        grid=(steps,),
        out_shape=(jax.ShapeDtypeStruct((1, LANES), f32), out, out, out),
        in_specs=[
            pl.BlockSpec((S, EXTRA, LANES), lambda i: (0, tok // EXTRA, 0)),
            smem(),
            smem(),
            pl.BlockSpec((group, None, tok, LANES), lambda i: (i, 0, 0, 0)),
            whole(1),
            whole(2),
            pl.BlockSpec((text, LANES), lambda i: (0, 0)),
            pl.BlockSpec((2, rows, seq_len), lambda i: (0, i, 0)),
            pl.BlockSpec((2, rows, text), lambda i: (0, i, 0)),
            pl.BlockSpec((rows, LANES), lambda i: (i, 0)),
            pl.BlockSpec((rows, LANES), lambda i: (i, 0)),
            block,
            pl.BlockSpec((group, tok + EXTRA, LANES), lambda i: (i, 0, 0)),
        ],
        out_specs=(
            pl.BlockSpec((1, LANES), lambda i: (0, 0)),
            pl.BlockSpec((None, 2, HEAD, rows), lambda i: (0, 0, 0, i)),
            full,
            full,
        ),
        scratch_shapes=[pltpu.VMEM((2, HEAD, seq_len), f32)] * 2,
        compiler_params=params,
        cost_estimate=cost(40 * seq_len * seq_len * LANES, e, e_text, qkv),
        name="backward_part",
    )(
        grads, steps_in, refs_in, qkv, qkv, qkv, ctx, in_hbm(e), in_hbm(e_text),
        *[in_hbm(x) for x in scales], attended, grads,
    )


def on_device(
    S, F, prompt, lengths, timesteps, ref_errors, gain_ffn, w_in_gate, w_in_up, w_in_down,
    gain_final, w_context, image_q, image_k, image_v, w_out, target,
):
    tok = image_q.shape[2]
    seq_len = S * tok
    if F == 2 and w_in_down.shape[1] == S * LANES:
        ctx, qkv, image, weights, w_idx = encode_shared(
            S, prompt, lengths, gain_ffn, w_in_gate, w_in_up, w_in_down, gain_final, w_context,
            w_out, (image_q[0], image_k[0], image_v[0]),
        )
        w_first = 3
    else:
        qkv = exchange(pack_heads(image_q[0], image_k[0], image_v[0])).reshape(S, 3, tok, LANES)
        ctx = encode_gathered(
            prompt, gain_ffn, w_in_gate, w_in_up, w_in_down, gain_final, w_context
        )
        image = image_part(qkv, 0, 1)
        weights = (lax.all_gather(w_out, "fsdp", axis=0, tiled=True),)
        w_idx, w_first = jnp.arange(F, dtype=jnp.int32), 0
    e_img, o_img, m_img, l_img = image

    attended, e_text, *scales = text_part(lengths, qkv, ctx, o_img, m_img, l_img)
    tokens = exchange(attended)
    grads = exchange(project(w_first, w_idx, tokens, target[0], weights))
    loss, grad_q, grad_k, grad_v = backward_part(
        seq_len * target.shape[-1], timesteps, ref_errors, qkv, ctx, e_img, e_text, scales,
        attended, grads,
    )
    turn = lambda x: jnp.swapaxes(x, 2, 3)
    return loss[0, :1], turn(grad_q), turn(grad_k), turn(grad_v)


def solution(mesh):
    S, F = mesh.shape["seq"], mesh.shape["fsdp"]

    def body(*args):
        return on_device(S, F, *args)

    return jax.shard_map(
        body,
        mesh=mesh,
        in_specs=(
            P("fsdp", None, None),
            P("fsdp"),
            P("fsdp"),
            P("fsdp", None),
            P(),
            P("fsdp", "seq"),
            P("fsdp", "seq"),
            P("seq", "fsdp"),
            P(),
            P("fsdp", "seq"),
            P("fsdp", None, "seq", None),
            P("fsdp", None, "seq", None),
            P("fsdp", None, "seq", None),
            P("fsdp", None),
            P("fsdp", None, "seq", None),
        ),
        out_specs=(
            P("fsdp"),
            P("fsdp", None, None, "seq"),
            P("fsdp", None, None, "seq"),
            P("fsdp", None, None, "seq"),
        ),
        check_vma=False,
    )
```
